32 devices in a mesh: dp: 8 (over z, x), tensor: 4 (over y, core).
Axes of the slice: x: 2, y: 2, z: 4, core: 2. Of those that a mesh axis runs over, the one named last changes fastest.
Arguments:
- tokens: bfloat16 [8, 1024, 1152], P('dp', 'tensor'), may hold values from -6 to 6
- conditioning: float32 [8, 1152], P('dp', 'tensor'), may hold values from -6 to 6
- out_grad: bfloat16 [8, 1024, 1152], P('dp', 'tensor'), may hold values from -6 to 6
- qkv_weight: float32 [3, 1152, 1152], P(None, 'dp', 'tensor'), may hold values from -0.1875 to 0.1875
- out_weight: float32 [1152, 1152], P('dp', 'tensor'), may hold values from -0.75 to 0.75
- up_weight: float32 [1152, 4608], P('dp', 'tensor'), may hold values from -0.1875 to 0.1875
- down_weight: float32 [1152, 4608], P('dp', 'tensor'), may hold values from -0.09375 to 0.09375
- ada_weight: float32 [6, 1152, 1152], P(None, 'dp', 'tensor'), may hold values from -0.1875 to 0.1875
- qkv_moment: float32 [3, 1152, 1152], P(None, 'dp', 'tensor'), may hold values from -0.00030517578 to 0.00030517578
- out_moment: float32 [1152, 1152], P('dp', 'tensor'), may hold values from -0.00030517578 to 0.00030517578
- up_moment: float32 [1152, 4608], P('dp', 'tensor'), may hold values from -0.00030517578 to 0.00030517578
- down_moment: float32 [1152, 4608], P('dp', 'tensor'), may hold values from -0.00030517578 to 0.00030517578
- ada_moment: float32 [6, 1152, 1152], P(None, 'dp', 'tensor'), may hold values from -0.00030517578 to 0.00030517578
- qkv_square: float32 [3, 1152, 1152], P(None, 'dp', 'tensor'), may hold values from 4.1862246e-11 to 1.6744899e-10
- out_square: float32 [1152, 1152], P('dp', 'tensor'), may hold values from 4.1862246e-11 to 1.6744899e-10
- up_square: float32 [1152, 4608], P('dp', 'tensor'), may hold values from 4.1862246e-11 to 1.6744899e-10
- down_square: float32 [1152, 4608], P('dp', 'tensor'), may hold values from 4.1862246e-11 to 1.6744899e-10
- ada_square: float32 [6, 1152, 1152], P(None, 'dp', 'tensor'), may hold values from 4.1862246e-11 to 1.6744899e-10
Outputs:
- block_out: bfloat16 [8, 1024, 1152], P('dp', 'tensor')
- input_grad: float32 [8, 1024, 1152], P('dp', 'tensor')
- cond_grad: float32 [8, 1152], P('dp', 'tensor')
- grad_norm: float32 [], replicated
- qkv_new: float32 [3, 1152, 1152], P(None, 'dp', 'tensor')
- out_new: float32 [1152, 1152], P('dp', 'tensor')
- up_new: float32 [1152, 4608], P('dp', 'tensor')
- down_new: float32 [1152, 4608], P('dp', 'tensor')
- ada_new: float32 [6, 1152, 1152], P(None, 'dp', 'tensor')
- qkv_moment_new: float32 [3, 1152, 1152], P(None, 'dp', 'tensor')
- out_moment_new: float32 [1152, 1152], P('dp', 'tensor')
- up_moment_new: float32 [1152, 4608], P('dp', 'tensor')
- down_moment_new: float32 [1152, 4608], P('dp', 'tensor')
- ada_moment_new: float32 [6, 1152, 1152], P(None, 'dp', 'tensor')
- qkv_square_new: float32 [3, 1152, 1152], P(None, 'dp', 'tensor')
- out_square_new: float32 [1152, 1152], P('dp', 'tensor')
- up_square_new: float32 [1152, 4608], P('dp', 'tensor')
- down_square_new: float32 [1152, 4608], P('dp', 'tensor')
- ada_square_new: float32 [6, 1152, 1152], P(None, 'dp', 'tensor')
The draws below stay inside these ranges and needn't reach their ends.
All inputs are finite; a program needn't handle non-finite values.
Results may differ from the reference program's by a relative error of at most 0.017.
The reference program's roundings to bfloat16 on the way count: a program that leaves them out, or rounds other values in their place, can miss the bound.
Values may be sent and summed in bfloat16 or wider, within the bound.
No kernel may reach another device: no remote copies, remote signals or barrier semaphores. Data moves between devices by JAX's collectives and lax.ppermute only.
A program may use at most 192 MiB of HBM per device.

```python
import math
import jax
import jax.numpy as jnp
from jax import lax

D = 1152
HEADS = 16
HEAD_DIM = 72
FF = 4608
SEQ = 1024
STEP = 10
LATENTS = 8


def steps_of(key, dims, shards, least, top_value):
    level, own = 1.0, jax.random.fold_in(key, 6)
    for position, blocks in shards:
        steps = jnp.exp(jax.random.uniform(jax.random.fold_in(own, position), (blocks,), jnp.float32, least / len(shards), top_value / len(shards)))
        level = level * jnp.repeat(steps, dims[position] // blocks).reshape([-1 if axis == position else 1 for axis in range(len(dims))])
    return level


def bell_draw(stream_key, extent, width, limit, shards=(), kind=jnp.bfloat16):
    gain = steps_of(stream_key, extent, shards, -0.22, 0.18) if shards else 1.0
    drawn = jax.random.normal(stream_key, extent, jnp.float32) * width * gain
    return jnp.minimum(jnp.maximum(drawn, -limit), limit).astype(kind)


def setup_inputs(seed: int = 0) -> dict:
    key_of = jax.random.split(jax.random.key(seed), 19)
    tokens = bell_draw(key_of[0], (LATENTS, SEQ, D), 1.0, 6.0, ((0, 8), (1, 4)))
    conditioning = bell_draw(key_of[1], (LATENTS, D), 1.0, 6.0, ((0, 8), (1, 4)), jnp.float32)
    out_grad = bell_draw(key_of[2], (LATENTS, SEQ, D), 1.0, 6.0, ((0, 8), (1, 4)))
    qkv_weight = bell_draw(key_of[3], (3, D, D), D ** -0.5, 0.1875, ((1, 8), (2, 4)), jnp.float32)
    out_weight = bell_draw(key_of[4], (D, D), (D // 16) ** -0.5, 0.75, ((0, 8), (1, 4)), jnp.float32)
    up_weight = bell_draw(key_of[5], (D, FF), D ** -0.5, 0.1875, ((0, 8), (1, 4)), jnp.float32)
    down_weight = bell_draw(key_of[6], (D, FF), FF ** -0.5, 0.09375, ((0, 8), (1, 4)), jnp.float32)
    ada_weight = bell_draw(key_of[7], (6, D, D), D ** -0.5, 0.1875, ((1, 8), (2, 4)), jnp.float32)
    qkv_moment = bell_draw(key_of[8], (3, D, D), (0.111 * (10 * D * D + 2 * D * FF) ** -0.5), 0.00030517578, ((1, 8), (2, 4)), jnp.float32)
    out_moment = bell_draw(key_of[9], (D, D), (0.111 * (10 * D * D + 2 * D * FF) ** -0.5), 0.00030517578, ((0, 8), (1, 4)), jnp.float32)
    up_moment = bell_draw(key_of[10], (D, FF), (0.111 * (10 * D * D + 2 * D * FF) ** -0.5), 0.00030517578, ((0, 8), (1, 4)), jnp.float32)
    down_moment = bell_draw(key_of[11], (D, FF), (0.111 * (10 * D * D + 2 * D * FF) ** -0.5), 0.00030517578, ((0, 8), (1, 4)), jnp.float32)
    ada_moment = bell_draw(key_of[12], (6, D, D), (0.111 * (10 * D * D + 2 * D * FF) ** -0.5), 0.00030517578, ((1, 8), (2, 4)), jnp.float32)
    qkv_square = jnp.clip(jnp.exp(math.log(1.674489852332428e-10) - 1.3862944 * jax.random.uniform(key_of[13], (3, D, D), jnp.float32) ** steps_of(key_of[13], (3, D, D), ((1, 8), (2, 4)), -0.2, 0.2)), 4.18622463083107e-11, 1.674489852332428e-10)
    out_square = jnp.clip(jnp.exp(math.log(1.674489852332428e-10) - 1.3862944 * jax.random.uniform(key_of[14], (D, D), jnp.float32) ** steps_of(key_of[14], (D, D), ((0, 8), (1, 4)), -0.2, 0.2)), 4.18622463083107e-11, 1.674489852332428e-10)
    up_square = jnp.clip(jnp.exp(math.log(1.674489852332428e-10) - 1.3862944 * jax.random.uniform(key_of[15], (D, FF), jnp.float32) ** steps_of(key_of[15], (D, FF), ((0, 8), (1, 4)), -0.2, 0.2)), 4.18622463083107e-11, 1.674489852332428e-10)
    down_square = jnp.clip(jnp.exp(math.log(1.674489852332428e-10) - 1.3862944 * jax.random.uniform(key_of[16], (D, FF), jnp.float32) ** steps_of(key_of[16], (D, FF), ((0, 8), (1, 4)), -0.2, 0.2)), 4.18622463083107e-11, 1.674489852332428e-10)
    ada_square = jnp.clip(jnp.exp(math.log(1.674489852332428e-10) - 1.3862944 * jax.random.uniform(key_of[17], (6, D, D), jnp.float32) ** steps_of(key_of[17], (6, D, D), ((1, 8), (2, 4)), -0.2, 0.2)), 4.18622463083107e-11, 1.674489852332428e-10)
    return {"tokens": tokens, "conditioning": conditioning, "out_grad": out_grad, "qkv_weight": qkv_weight, "out_weight": out_weight, "up_weight": up_weight, "down_weight": down_weight, "ada_weight": ada_weight, "qkv_moment": qkv_moment, "out_moment": out_moment, "up_moment": up_moment, "down_moment": down_moment, "ada_moment": ada_moment, "qkv_square": qkv_square, "out_square": out_square, "up_square": up_square, "down_square": down_square, "ada_square": ada_square}


EPS_NORM = 1e-06
CLIP_NORM = 1.0
LEARN_RATE = 0.05
WEIGHT_DECAY = 0.1
BETA_ONE = 0.9
BETA_TWO = 0.999
EPS_ADAM = 1e-08
HIGHEST_PRECISION = lax.Precision.HIGHEST

@jax.custom_vjp
def low(v):
    return lax.optimization_barrier(v.astype(jnp.bfloat16)).astype(jnp.float32)

@jax.custom_vjp
def low_back(v):
    return v

def low_keep(v):
    return (low(v), None)

def low_pass(kept, grad):
    return (grad,)

def back_keep(v):
    return (v, None)

def back_low(kept, grad):
    return (low(grad),)
low.defvjp(low_keep, low_pass)
low_back.defvjp(back_keep, back_low)

def layer_norm(values):
    centre = values - lax.optimization_barrier(jnp.mean(values, axis=-1, keepdims=True))
    spread = lax.optimization_barrier(jnp.mean(centre * centre, axis=-1, keepdims=True))
    return centre * lax.rsqrt(spread + EPS_NORM)

def attend(queries, key_rows, values):
    block_rows = min(512, SEQ)
    score_scale = HEAD_DIM ** (-0.5)
    latents_here = queries.shape[0]
    blocked = jnp.moveaxis(queries.reshape(latents_here, SEQ // block_rows, block_rows, HEADS, HEAD_DIM), 1, 0)

    def one_block(query_part):
        scores = low_back(jnp.einsum('bqhe,bkhe->bhqk', query_part, key_rows, precision=HIGHEST_PRECISION) * score_scale)
        row_peak = lax.optimization_barrier(jnp.max(scores, axis=-1, keepdims=True))
        exponent = jnp.exp(scores - row_peak)
        probability = exponent / lax.optimization_barrier(jnp.sum(exponent, axis=-1, keepdims=True))
        return jnp.einsum('bhqk,bkhe->bqhe', low(probability), values, precision=HIGHEST_PRECISION)
    mixture = lax.map(jax.checkpoint(one_block), blocked)
    return jnp.moveaxis(mixture, 0, 1).reshape(queries.shape)

def forward(residual, conditioning, qkv_weight, out_weight, up_weight, down_weight, ada_weight):
    latents_here = residual.shape[0]
    signal = low(jax.nn.silu(conditioning))
    modulation = low_back(jnp.einsum('bi,kni->bkn', signal, low(ada_weight), precision=HIGHEST_PRECISION))
    shift_one = modulation[:, 0, None, :]
    scale_one = modulation[:, 1, None, :]
    gate_one = modulation[:, 2, None, :]
    shift_two = modulation[:, 3, None, :]
    scale_two = modulation[:, 4, None, :]
    gate_two = modulation[:, 5, None, :]
    normed_one = low(layer_norm(residual) * (1.0 + scale_one) + shift_one)
    projected = low(low_back(jnp.einsum('bsd,tde->tbse', normed_one, low(qkv_weight), precision=HIGHEST_PRECISION)))
    heads_split = projected.reshape(3, latents_here, SEQ, HEADS, HEAD_DIM)
    mixture = attend(heads_split[0], heads_split[1], heads_split[2]).reshape(latents_here, SEQ, D)
    attended = low(low_back(mixture))
    attn_rows = low_back(jnp.einsum('bse,de->bsd', attended, low(out_weight), precision=HIGHEST_PRECISION))
    middle = residual + gate_one * attn_rows
    normed_two = low(layer_norm(middle) * (1.0 + scale_two) + shift_two)
    pre_act = low_back(jnp.einsum('bsd,df->bsf', normed_two, low(up_weight), precision=HIGHEST_PRECISION))
    hidden = low(jax.nn.gelu(pre_act, approximate=True))
    mlp_rows = low_back(jnp.einsum('bsf,df->bsd', hidden, low(down_weight), precision=HIGHEST_PRECISION))
    return middle + gate_two * mlp_rows

def adam_update(weight, gradient, moment, square, clip_factor):
    clipped = gradient * clip_factor
    moment_new = BETA_ONE * moment + (1.0 - BETA_ONE) * clipped
    square_new = BETA_TWO * square + (1.0 - BETA_TWO) * clipped * clipped
    mean_hat = moment_new / (1.0 - BETA_ONE ** STEP)
    square_hat = square_new / (1.0 - BETA_TWO ** STEP)
    weight_new = weight - LEARN_RATE * (mean_hat / (jnp.sqrt(square_hat) + EPS_ADAM) + WEIGHT_DECAY * weight)
    return (weight_new, moment_new, square_new)

def reference(tokens, conditioning, out_grad, qkv_weight, out_weight, up_weight, down_weight, ada_weight, qkv_moment, out_moment, up_moment, down_moment, ada_moment, qkv_square, out_square, up_square, down_square, ada_square):
    group_size = math.gcd(LATENTS, max(1, 4096 // SEQ))
    group_count = LATENTS // group_size
    tokens_grouped = tokens.astype(jnp.float32).reshape(group_count, group_size, SEQ, D)
    cond_grouped = conditioning.reshape(group_count, group_size, D)
    grad_grouped = out_grad.astype(jnp.float32).reshape(group_count, group_size, SEQ, D)

    def accumulate(running, sample):
        block_in, cond_in, grad_in = sample
        result, pullback = jax.vjp(forward, block_in, cond_in, qkv_weight, out_weight, up_weight, down_weight, ada_weight)
        gradients = pullback(grad_in)
        running = (running[0] + gradients[2], running[1] + gradients[3], running[2] + gradients[4], running[3] + gradients[5], running[4] + gradients[6])
        return (running, (result.astype(jnp.bfloat16), gradients[0], gradients[1]))
    zero_sums = (jnp.zeros_like(qkv_weight), jnp.zeros_like(out_weight), jnp.zeros_like(up_weight), jnp.zeros_like(down_weight), jnp.zeros_like(ada_weight))
    running, (outputs, input_grads, cond_grads) = lax.scan(accumulate, zero_sums, (tokens_grouped, cond_grouped, grad_grouped))
    squares = jnp.sum(running[0] * running[0]) + jnp.sum(running[1] * running[1]) + jnp.sum(running[2] * running[2])
    squares = squares + jnp.sum(running[3] * running[3]) + jnp.sum(running[4] * running[4])
    grad_norm = jnp.sqrt(squares)
    clip_factor = CLIP_NORM / jnp.maximum(grad_norm, CLIP_NORM)
    qkv_new, qkv_moment_new, qkv_square_new = adam_update(qkv_weight, running[0], qkv_moment, qkv_square, clip_factor)
    out_new, out_moment_new, out_square_new = adam_update(out_weight, running[1], out_moment, out_square, clip_factor)
    up_new, up_moment_new, up_square_new = adam_update(up_weight, running[2], up_moment, up_square, clip_factor)
    down_new, down_moment_new, down_square_new = adam_update(down_weight, running[3], down_moment, down_square, clip_factor)
    ada_new, ada_moment_new, ada_square_new = adam_update(ada_weight, running[4], ada_moment, ada_square, clip_factor)
    return (outputs.reshape(LATENTS, SEQ, D), input_grads.reshape(LATENTS, SEQ, D), cond_grads.reshape(LATENTS, D), grad_norm, qkv_new, out_new, up_new, down_new, ada_new, qkv_moment_new, out_moment_new, up_moment_new, down_moment_new, ada_moment_new, qkv_square_new, out_square_new, up_square_new, down_square_new, ada_square_new)
```

```python
import jax
import jax.numpy as jnp
import numpy as np
from jax import lax
from jax.sharding import PartitionSpec as P

HEAD_DIM = 72
STEP = 10

EPS_NORM = 1e-06
CLIP_NORM = 1.0
LEARN_RATE = 0.05
WEIGHT_DECAY = 0.1
BETA_ONE = 0.9
BETA_TWO = 0.999
EPS_ADAM = 1e-08

LOW = jnp.bfloat16
WIDE = jnp.float32


def bit_count(size):
    return size.bit_length() - 1


def flip(value, axis, size, bit):
    return lax.ppermute(value, axis, [(i, i ^ (1 << bit)) for i in range(size)])


def gather_rel(value, axis, size):
    for bit in reversed(range(bit_count(size))):
        value = jnp.concatenate([value, flip(value, axis, size, bit)], axis=0)
    return value


def scatter_rel(value, axis, size):
    for bit in range(bit_count(size)):
        half = value.shape[0] // 2
        moved = flip(value[half:].astype(LOW), axis, size, bit)
        value = value[:half] + moved.astype(WIDE)
    return value


def exchange_rel(value, axis, size):
    lead = 1
    value = value[None]
    for bit in range(bit_count(size)):
        half = value.shape[1] // 2
        moved = flip(value[:, half:], axis, size, bit)
        value = jnp.stack([value[:, :half], moved], axis=1)
        lead *= 2
        value = value.reshape((lead, half) + value.shape[3:])
    return value[:, 0]


def sum_all(value, axis, size):
    for bit in range(bit_count(size)):
        value = value + flip(value, axis, size, bit)
    return value


def reversed_bits(size):
    bits = bit_count(size)
    return np.array([int(format(i, f"0{bits}b")[::-1], 2) if bits else 0 for i in range(size)])


def selection(index, size, width):
    block = width // size
    place = np.arange(width)
    source = (index ^ jnp.asarray(reversed_bits(size)[place // block], jnp.int32)) * block
    source = source + jnp.asarray(place % block, jnp.int32)
    return (lax.broadcasted_iota(jnp.int32, (width, width), 0) == source[None, :]).astype(LOW)


def matmul(left, right, dims):
    return lax.dot_general(left, right, (dims, ((), ())), preferred_element_type=WIDE)


def normalize(values):
    centre = values - jnp.mean(values, axis=-1, keepdims=True)
    spread = jnp.mean(centre * centre, axis=-1, keepdims=True)
    inverse = lax.rsqrt(spread + EPS_NORM)
    return centre * inverse, inverse


def normalize_back(normed, inverse, grad):
    mean_grad = jnp.mean(grad, axis=-1, keepdims=True)
    mean_both = jnp.mean(grad * normed, axis=-1, keepdims=True)
    return inverse * (grad - mean_grad - normed * mean_both)


def gelu_tanh(values):
    return jax.nn.gelu(values, approximate=True)


def to_blocks(stacked, block_rows):
    return stacked.reshape((-1, block_rows) + stacked.shape[1:])


def attend(queries, key_rows, values, block_rows):
    score_scale = HEAD_DIM ** (-0.5)

    def forward_block(query_part):
        scores = (
            jnp.einsum("qhe,khe->hqk", query_part, key_rows, preferred_element_type=WIDE)
            * score_scale
        )
        row_peak = jnp.max(scores, axis=-1, keepdims=True)
        exponent = jnp.exp(scores - row_peak)
        row_total = jnp.sum(exponent, axis=-1, keepdims=True)
        probability = (exponent / row_total).astype(LOW)
        mixture = jnp.einsum("hqk,khe->qhe", probability, values, preferred_element_type=WIDE)
        return (mixture.astype(LOW), (row_peak + jnp.log(row_total))[..., 0])

    mixed, log_totals = lax.map(forward_block, to_blocks(queries, block_rows))
    return mixed.reshape(queries.shape), log_totals


def attend_back(queries, key_rows, values, log_totals, grad_attended, block_rows):
    score_scale = HEAD_DIM ** (-0.5)

    def backward_block(carried, sample):
        grad_keys, grad_values = carried
        query_part, grad_part, log_part = sample
        scores = (
            jnp.einsum("qhe,khe->hqk", query_part, key_rows, preferred_element_type=WIDE)
            * score_scale
        )
        probability = jnp.exp(scores - log_part[..., None])
        grad_probability = jnp.einsum(
            "qhe,khe->hqk", grad_part, values, preferred_element_type=WIDE
        )
        row_inner = jnp.sum(probability * grad_probability, axis=-1, keepdims=True)
        grad_scores = (probability * (grad_probability - row_inner)).astype(LOW)
        grad_query = (
            jnp.einsum("hqk,khe->qhe", grad_scores, key_rows, preferred_element_type=WIDE)
            * score_scale
        )
        grad_keys = (
            grad_keys
            + jnp.einsum("hqk,qhe->khe", grad_scores, query_part, preferred_element_type=WIDE)
            * score_scale
        )
        grad_values = grad_values + jnp.einsum(
            "hqk,qhe->khe", probability.astype(LOW), grad_part, preferred_element_type=WIDE
        )
        return ((grad_keys, grad_values), grad_query.astype(LOW))

    zero_grad = jnp.zeros(key_rows.shape, WIDE)
    (grad_keys, grad_values), grad_queries = lax.scan(
        backward_block,
        (zero_grad, zero_grad),
        (to_blocks(queries, block_rows), to_blocks(grad_attended, block_rows), log_totals),
    )
    return (
        grad_queries.reshape(queries.shape),
        grad_keys.astype(LOW),
        grad_values.astype(LOW),
    )


def adam_update(weight, gradient, moment, square, clip_factor):
    clipped = gradient * clip_factor
    moment_new = BETA_ONE * moment + (1.0 - BETA_ONE) * clipped
    square_new = BETA_TWO * square + (1.0 - BETA_TWO) * clipped * clipped
    mean_hat = moment_new / (1.0 - BETA_ONE**STEP)
    square_hat = square_new / (1.0 - BETA_TWO**STEP)
    weight_new = weight - LEARN_RATE * (
        mean_hat / (jnp.sqrt(square_hat) + EPS_ADAM) + WEIGHT_DECAY * weight
    )
    return (weight_new, moment_new, square_new)


def on_device(
    dp,
    tp,
    tokens,
    conditioning,
    out_grad,
    qkv_weight,
    out_weight,
    up_weight,
    down_weight,
    ada_weight,
    qkv_moment,
    out_moment,
    up_moment,
    down_moment,
    ada_moment,
    qkv_square,
    out_square,
    up_square,
    down_square,
    ada_square,
):
    width = tokens.shape[-1]
    own_rows = tokens.shape[1]
    heads_width = out_weight.shape[-1]
    here = lax.axis_index("dp")
    select = selection(here, dp, width)

    both = jnp.concatenate(
        [
            matmul(tokens[0], select, ((1,), (0,))).astype(LOW),
            matmul(out_grad[0], select, ((1,), (0,))).astype(LOW),
        ],
        axis=1,
    )
    both = gather_rel(both, "tensor", tp)
    tokens_all = both[:, :width].astype(WIDE)
    grad_all = both[:, width:].astype(WIDE)

    low_qkv = jnp.moveaxis(qkv_weight.astype(LOW), 0, 1).reshape(qkv_weight.shape[1], -1)
    full_qkv = gather_rel(low_qkv, "dp", dp)
    full_out = gather_rel(out_weight.astype(LOW), "dp", dp)
    full_up = gather_rel(up_weight.astype(LOW), "dp", dp)
    full_down = gather_rel(down_weight.astype(LOW), "dp", dp)
    low_ada = ada_weight.astype(LOW)

    signal, silu_back = jax.vjp(jax.nn.silu, conditioning)
    signal_all = gather_rel(signal.astype(LOW), "dp", dp)
    mod_terms = jnp.einsum("pi,kni->pkn", signal_all, low_ada, preferred_element_type=WIDE)
    mod_terms = sum_all(mod_terms, "tensor", tp)
    modulation = exchange_rel(mod_terms, "dp", dp)
    modulation = jnp.moveaxis(modulation, 0, 1).reshape(6, 1, width)
    shift_one, scale_one, gate_one, shift_two, scale_two, gate_two = modulation

    norm_one, inverse_one = normalize(tokens_all)
    normed_one = (norm_one * (1.0 + scale_one) + shift_one).astype(LOW)
    projected = matmul(normed_one, full_qkv, ((1,), (0,))).astype(LOW)
    length = projected.shape[0]
    block_rows = min(512, length)
    heads_split = projected.reshape(length, 3, heads_width // HEAD_DIM, HEAD_DIM)
    queries, key_rows, values = heads_split[:, 0], heads_split[:, 1], heads_split[:, 2]
    mixed, log_totals = attend(queries, key_rows, values, block_rows)
    attended = mixed.reshape(length, heads_width)
    attn_terms = matmul(attended, full_out, ((1,), (1,)))

    def sum_half(terms):
        half = terms.shape[0] // 2
        total = terms[:half] + flip(terms[half:].astype(LOW), "tensor", tp, 0).astype(WIDE)
        for bit in range(1, bit_count(tp)):
            sent = total.astype(LOW)
            moved = flip(sent, "tensor", tp, bit)
            blocks = moved.reshape((-1, 2, own_rows << (bit_count(tp) - 1 - bit), width))
            moved = blocks[:, ::-1].reshape(moved.shape)
            total = sent.astype(WIDE) + moved.astype(WIDE)
        return total

    half = length // 2
    attn_rows = sum_half(attn_terms)
    middle = tokens_all[:half] + gate_one * attn_rows
    norm_two, inverse_two = normalize(middle)
    normed_two = (norm_two * (1.0 + scale_two) + shift_two).astype(LOW)
    seq_two = jnp.concatenate([normed_two, flip(normed_two, "tensor", tp, 0)], axis=0)

    pre_act = matmul(seq_two, full_up, ((1,), (0,)))
    activated, gelu_back = jax.vjp(gelu_tanh, pre_act)
    hidden = activated.astype(LOW)
    mlp_terms = matmul(hidden, full_down, ((1,), (1,)))
    mlp_rows = scatter_rel(mlp_terms, "tensor", tp)
    block_out = (middle[:own_rows] + gate_two * mlp_rows).astype(LOW)
    block_out = matmul(block_out, select, ((1,), (1,))).astype(LOW)
    grad_gate_two = jnp.sum(grad_all[:own_rows] * mlp_rows, axis=0)

    grad_mlp = (grad_all * gate_two).astype(LOW)
    grad_down = matmul(grad_mlp, hidden, ((0,), (0,)))
    grad_hidden = matmul(grad_mlp, full_down, ((1,), (0,)))
    grad_pre = gelu_back(grad_hidden)[0].astype(LOW)
    grad_up = matmul(seq_two, grad_pre, ((0,), (0,)))
    grad_two_terms = matmul(grad_pre, full_up, ((1,), (1,)))
    summed_down = scatter_rel(grad_down, "dp", dp)
    summed_up = scatter_rel(grad_up, "dp", dp)
    grad_normed_two = sum_half(grad_two_terms)
    grad_shift_two = jnp.sum(grad_normed_two[:own_rows], axis=0)
    grad_scale_two = jnp.sum((grad_normed_two * norm_two)[:own_rows], axis=0)
    grad_middle = grad_all[:half] + normalize_back(
        norm_two, inverse_two, grad_normed_two * (1.0 + scale_two)
    )
    grad_gate_one = jnp.sum((grad_middle * attn_rows)[:own_rows], axis=0)

    grad_attn = (grad_middle * gate_one).astype(LOW)
    grad_attn = jnp.concatenate([grad_attn, flip(grad_attn, "tensor", tp, 0)], axis=0)
    grad_out = matmul(grad_attn, attended, ((0,), (0,)))
    summed_out = scatter_rel(grad_out, "dp", dp)
    grad_attended = matmul(grad_attn, full_out, ((1,), (0,))).astype(LOW)
    grad_parts = attend_back(
        queries, key_rows, values, log_totals, grad_attended.reshape(queries.shape), block_rows
    )
    grad_projected = jnp.stack(grad_parts, axis=1).reshape(length, 3 * heads_width)
    grad_qkv = matmul(normed_one, grad_projected, ((0,), (0,)))
    summed_qkv = scatter_rel(grad_qkv, "dp", dp)
    grad_one_terms = matmul(grad_projected, full_qkv, ((1,), (1,)))
    grad_normed_one = scatter_rel(grad_one_terms, "tensor", tp)
    input_grad = grad_middle[:own_rows] + normalize_back(
        norm_one[:own_rows], inverse_one[:own_rows], grad_normed_one * (1.0 + scale_one)
    )
    coarse = input_grad.astype(LOW)
    fine = (input_grad - coarse.astype(WIDE)).astype(LOW)
    input_grad = matmul(coarse, select, ((1,), (1,))) + matmul(fine, select, ((1,), (1,)))

    grad_shift_one = jnp.sum(grad_one_terms, axis=0)
    grad_scale_one = jnp.sum(grad_one_terms * norm_one, axis=0)
    grad_mod = jnp.stack(
        [
            grad_shift_one,
            grad_scale_one,
            grad_gate_one,
            grad_shift_two,
            grad_scale_two,
            grad_gate_two,
        ]
    )
    grad_mod = sum_all(grad_mod, "tensor", tp).astype(LOW)
    grad_mod = jnp.moveaxis(grad_mod.reshape(6, dp, width // dp), 1, 0)
    grad_mod = exchange_rel(grad_mod, "dp", dp)
    summed_ada = jnp.einsum("pkn,pi->kni", grad_mod, signal_all, preferred_element_type=WIDE)
    grad_signal = jnp.einsum("pkn,kni->pi", grad_mod, low_ada, preferred_element_type=WIDE)
    for bit in range(bit_count(dp)):
        part = grad_signal.shape[0] // 2
        grad_signal = grad_signal[:part] + flip(grad_signal[part:], "dp", dp, bit)
    cond_grad = silu_back(grad_signal)[0]

    summed_qkv = jnp.moveaxis(summed_qkv.reshape(-1, 3, heads_width), 1, 0)
    total = jnp.sum(summed_qkv * summed_qkv) + jnp.sum(summed_out * summed_out)
    total = total + jnp.sum(summed_up * summed_up) + jnp.sum(summed_down * summed_down)
    total = total + jnp.sum(summed_ada * summed_ada)
    total = sum_all(sum_all(total, "tensor", tp), "dp", dp)
    grad_norm = jnp.sqrt(total)
    clip_factor = CLIP_NORM / jnp.maximum(grad_norm, CLIP_NORM)
    qkv = adam_update(qkv_weight, summed_qkv, qkv_moment, qkv_square, clip_factor)
    out = adam_update(out_weight, summed_out, out_moment, out_square, clip_factor)
    up = adam_update(up_weight, summed_up, up_moment, up_square, clip_factor)
    down = adam_update(down_weight, summed_down, down_moment, down_square, clip_factor)
    ada = adam_update(ada_weight, summed_ada, ada_moment, ada_square, clip_factor)
    return (
        block_out[None],
        input_grad[None],
        cond_grad,
        grad_norm,
        *(new for group in zip(qkv, out, up, down, ada) for new in group),
    )


def solution(mesh):
    dp, tp = mesh.shape["dp"], mesh.shape["tensor"]
    rows = P("dp", "tensor", None)
    plain = P("dp", "tensor")
    stacked = P(None, "dp", "tensor")
    weights = (stacked, plain, plain, plain, stacked)

    def step(*arrays):
        return on_device(dp, tp, *arrays)

    return jax.shard_map(
        step,
        mesh=mesh,
        in_specs=(rows, plain, rows) + weights * 3,
        out_specs=(rows, rows, plain, P()) + weights * 3,
        check_vma=False,
    )
```

```python
import jax
import jax.numpy as jnp
import numpy as np
from jax import lax
from jax.sharding import PartitionSpec as P

HEAD_DIM = 72
STEP = 10

EPS_NORM = 1e-06
CLIP_NORM = 1.0
LEARN_RATE = 0.05
WEIGHT_DECAY = 0.1
BETA_ONE = 0.9
BETA_TWO = 0.999
EPS_ADAM = 1e-08

LOW = jnp.bfloat16
WIDE = jnp.float32


def bit_count(size):
    return size.bit_length() - 1


def flip(value, axis, size, bit):
    return lax.ppermute(value, axis, [(i, i ^ (1 << bit)) for i in range(size)])


def grow(value, axis, size, bit):
    return jnp.concatenate([value, flip(value, axis, size, bit)], axis=0)


def shrink(value, axis, size, bit):
    half = value.shape[0] // 2
    moved = flip(value[half:].astype(LOW), axis, size, bit)
    return value[:half] + moved.astype(WIDE)


def gather_rel(value, axis, size):
    for bit in reversed(range(bit_count(size))):
        value = grow(value, axis, size, bit)
    return value


def scatter_rel(value, axis, size):
    for bit in range(bit_count(size)):
        value = shrink(value, axis, size, bit)
    return value


def spread_features(value, axis, size, bit):
    pairs = value.reshape((value.shape[0] // 2, 2) + value.shape[1:])
    moved = flip(pairs[:, 1], axis, size, bit)
    return jnp.concatenate([pairs[:, 0], moved], axis=-1)


def fold_features(value, axis, size):
    value = value[None]
    for bit in range(bit_count(size)):
        half = value.shape[-1] // 2
        moved = flip(value[..., half:], axis, size, bit)
        value = jnp.stack([value[..., :half], moved], axis=1)
        value = value.reshape((-1,) + value.shape[2:])
    return value


def sum_all(value, axis, size):
    for bit in range(bit_count(size)):
        value = value + flip(value, axis, size, bit)
    return value


def pin(*values):
    return lax.optimization_barrier(values)


def reversed_bits(size):
    bits = bit_count(size)
    return np.array([int(format(i, f"0{bits}b")[::-1], 2) if bits else 0 for i in range(size)])


def selection(index, size, width):
    block = width // size
    place = np.arange(width)
    source = (index ^ jnp.asarray(reversed_bits(size)[place // block], jnp.int32)) * block
    source = source + jnp.asarray(place % block, jnp.int32)
    return (lax.broadcasted_iota(jnp.int32, (width, width), 0) == source[None, :]).astype(LOW)


def matmul(left, right, dims):
    return lax.dot_general(left, right, (dims, ((), ())), preferred_element_type=WIDE)


def normalize(values):
    centre = values - jnp.mean(values, axis=-1, keepdims=True)
    spread = jnp.mean(centre * centre, axis=-1, keepdims=True)
    inverse = lax.rsqrt(spread + EPS_NORM)
    return centre * inverse, inverse


def normalize_back(normed, inverse, grad):
    mean_grad = jnp.mean(grad, axis=-1, keepdims=True)
    mean_both = jnp.mean(grad * normed, axis=-1, keepdims=True)
    return inverse * (grad - mean_grad - normed * mean_both)


def gelu_tanh(values):
    return jax.nn.gelu(values, approximate=True)


def attend(queries, key_rows, values):
    score_scale = HEAD_DIM ** (-0.5)
    scores = (
        jnp.einsum("qhe,khe->hqk", queries, key_rows, preferred_element_type=WIDE) * score_scale
    )
    row_peak = jnp.max(scores, axis=-1, keepdims=True)
    exponent = jnp.exp(scores - row_peak)
    row_total = jnp.sum(exponent, axis=-1, keepdims=True)
    probability = (exponent / row_total).astype(LOW)
    mixture = jnp.einsum("hqk,khe->qhe", probability, values, preferred_element_type=WIDE)
    return mixture.astype(LOW), row_peak + jnp.log(row_total)


def attend_back(queries, key_rows, values, log_total, grad_attended):
    score_scale = HEAD_DIM ** (-0.5)
    scores = (
        jnp.einsum("qhe,khe->hqk", queries, key_rows, preferred_element_type=WIDE) * score_scale
    )
    probability = jnp.exp(scores - log_total)
    grad_probability = jnp.einsum("qhe,khe->hqk", grad_attended, values, preferred_element_type=WIDE)
    row_inner = jnp.sum(probability * grad_probability, axis=-1, keepdims=True)
    grad_scores = (probability * (grad_probability - row_inner)).astype(LOW)
    grad_query = (
        jnp.einsum("hqk,khe->qhe", grad_scores, key_rows, preferred_element_type=WIDE) * score_scale
    )
    grad_keys = (
        jnp.einsum("hqk,qhe->khe", grad_scores, queries, preferred_element_type=WIDE) * score_scale
    )
    grad_values = jnp.einsum(
        "hqk,qhe->khe", probability.astype(LOW), grad_attended, preferred_element_type=WIDE
    )
    return grad_query.astype(LOW), grad_keys, grad_values


def adam_update(weight, gradient, moment, square, clip_factor):
    clipped = gradient * clip_factor
    moment_new = BETA_ONE * moment + (1.0 - BETA_ONE) * clipped
    square_new = BETA_TWO * square + (1.0 - BETA_TWO) * clipped * clipped
    mean_hat = moment_new / (1.0 - BETA_ONE**STEP)
    square_hat = square_new / (1.0 - BETA_TWO**STEP)
    weight_new = weight - LEARN_RATE * (
        mean_hat / (jnp.sqrt(square_hat) + EPS_ADAM) + WEIGHT_DECAY * weight
    )
    return (weight_new, moment_new, square_new)


def on_device(
    dp,
    tp,
    tokens,
    conditioning,
    out_grad,
    qkv_weight,
    out_weight,
    up_weight,
    down_weight,
    ada_weight,
    qkv_moment,
    out_moment,
    up_moment,
    down_moment,
    ada_moment,
    qkv_square,
    out_square,
    up_square,
    down_square,
    ada_square,
):
    width = tokens.shape[-1]
    heads_width = out_weight.shape[-1]
    here = lax.axis_index("dp")
    select = selection(here, dp, width)
    low_bits = bit_count(dp)
    high_bits = range(1, bit_count(tp))
    chunks = range(tp // 2)

    def swap(value, bit):
        return flip(value, "tensor", tp, bit)

    def widen(value):
        return jnp.concatenate([value, swap(value, 0)], axis=0)

    def all_blocks(value):
        pieces = [value]
        for bit in reversed(high_bits):
            pieces = pieces + [swap(piece, bit) for piece in pieces]
        return pieces

    def token_sum(kept, sent):
        part = [keep + swap(send, 0).astype(WIDE) for keep, send in zip(kept, sent)]
        for bit in high_bits:
            low_part = [value.astype(LOW) for value in part]
            moved = [swap(value, bit) for value in low_part]
            part = [
                low_part[k].astype(WIDE) + moved[k ^ (1 << (bit - 1))].astype(WIDE) for k in chunks
            ]
        return part

    def split_product(left, right, dims):
        rows = left.shape[0] // 2
        return pin(matmul(left[:rows], right, dims), matmul(left[rows:], right, dims).astype(LOW))

    signal, silu_back = jax.vjp(jax.nn.silu, conditioning)
    signal_all = gather_rel(signal.astype(LOW), "dp", dp)
    low_ada = ada_weight.astype(LOW)
    own_tokens = matmul(tokens[0], select, ((1,), (0,))).astype(LOW)
    own_grad = matmul(out_grad[0], select, ((1,), (0,))).astype(LOW)
    tokens_low = [widen(piece) for piece in all_blocks(own_tokens)]
    full_qkv = jnp.concatenate([qkv_weight[t].astype(LOW) for t in range(3)], axis=1)
    full_qkv = grow(full_qkv, "dp", dp, low_bits - 1)
    modulation = jnp.einsum("pi,kni->pkn", signal_all, low_ada, preferred_element_type=WIDE)
    modulation = sum_all(modulation, "tensor", tp)
    full_qkv, modulation = pin(full_qkv, modulation)
    full_up = out_weight.astype(LOW), up_weight.astype(LOW), down_weight.astype(LOW)
    full_out, full_up, full_down = (grow(w, "dp", dp, low_bits - 1) for w in full_up)
    for bit in reversed(range(1, low_bits)):
        modulation = spread_features(modulation, "dp", dp, bit)
    for bit in reversed(range(1, low_bits - 1)):
        full_qkv = grow(full_qkv, "dp", dp, bit)
    full_qkv, modulation, full_out, full_up = pin(full_qkv, modulation, full_out, full_up)
    modulation = spread_features(modulation, "dp", dp, 0)
    full_qkv = grow(full_qkv, "dp", dp, 0)
    for bit in reversed(range(1, low_bits - 1)):
        full_out = grow(full_out, "dp", dp, bit)
        full_up = grow(full_up, "dp", dp, bit)
    modulation = modulation.reshape(6, 1, width)
    shift_one, scale_one, gate_one, shift_two, scale_two, gate_two = modulation

    tokens_wide = [value.astype(WIDE) for value in tokens_low]
    norm_one, inverse_one = zip(*(pin(*normalize(value)) for value in tokens_wide))
    normed_one = [(value * (1.0 + scale_one) + shift_one).astype(LOW) for value in norm_one]
    normed_one = jnp.concatenate(normed_one, axis=0)
    normed_one, full_qkv, full_down = pin(normed_one, full_qkv, full_down)
    for bit in reversed(range(1, low_bits - 1)):
        full_down = grow(full_down, "dp", dp, bit)
    projected = matmul(normed_one, full_qkv, ((1,), (0,))).astype(LOW)
    projected, full_out, full_up = pin(projected, full_out, full_up)
    full_out = grow(full_out, "dp", dp, 0)
    full_up = grow(full_up, "dp", dp, 0)
    grad_low = [widen(piece) for piece in all_blocks(own_grad)]
    length = projected.shape[0]
    heads_split = projected.reshape(length, 3, heads_width // HEAD_DIM, HEAD_DIM)
    queries, key_rows, values = heads_split[:, 0], heads_split[:, 1], heads_split[:, 2]
    chunk_rows = length // len(chunks)
    query_parts = [queries[k * chunk_rows : (k + 1) * chunk_rows] for k in chunks]
    mixed, log_totals = zip(*(attend(part, key_rows, values) for part in query_parts))
    attended = [part.reshape(chunk_rows, heads_width) for part in mixed]
    attended[0], full_out, full_down = pin(attended[0], full_out, full_down)
    attn_terms = zip(*(split_product(part, full_out, ((1,), (1,))) for part in attended))
    attn_rows = token_sum(*attn_terms)
    own_rows = attn_rows[0].shape[0]
    middle = [tokens_wide[k][:own_rows] + gate_one * attn_rows[k] for k in chunks]
    norm_two, inverse_two = zip(*(normalize(value) for value in middle))
    normed_two = [(value * (1.0 + scale_two) + shift_two).astype(LOW) for value in norm_two]
    normed_two[0], full_up = pin(normed_two[0], full_up)
    full_down = grow(full_down, "dp", dp, 0)
    seq_two = [widen(value) for value in normed_two]

    pre_act = [matmul(part, full_up, ((1,), (0,))) for part in seq_two]
    activated, gelu_back = zip(*(jax.vjp(gelu_tanh, part) for part in pre_act))
    hidden = [part.astype(LOW) for part in activated]

    grad_mlp = [(part.astype(WIDE) * gate_two).astype(LOW) for part in grad_low]
    grad_hidden = [matmul(part, full_down, ((1,), (0,))) for part in grad_mlp]
    grad_pre = [back(part)[0].astype(LOW) for back, part in zip(gelu_back, grad_hidden)]
    grad_terms = zip(*(split_product(part, full_up, ((1,), (1,))) for part in grad_pre))
    grad_normed_two = token_sum(*grad_terms)
    all_hidden = jnp.concatenate(hidden, axis=0)
    grad_down = matmul(jnp.concatenate(grad_mlp, axis=0), all_hidden, ((0,), (0,)))
    summed_down = scatter_rel(grad_down, "dp", dp)
    all_seq_two = jnp.concatenate(seq_two, axis=0)
    grad_up = matmul(all_seq_two, jnp.concatenate(grad_pre, axis=0), ((0,), (0,)))
    summed_up = scatter_rel(grad_up, "dp", dp)

    mlp_kept, mlp_sent = zip(*(split_product(part, full_down, ((1,), (1,))) for part in hidden))
    mlp_part = [keep + swap(send, 0).astype(WIDE) for keep, send in zip(mlp_kept, mlp_sent)]
    for bit in high_bits:
        mlp_part = [
            mlp_part[2 * k] + swap(mlp_part[2 * k + 1].astype(LOW), bit).astype(WIDE)
            for k in range(len(mlp_part) // 2)
        ]
    mlp_rows = mlp_part[0]
    block_out = (middle[0] + gate_two * mlp_rows).astype(LOW)
    block_out = matmul(block_out, select, ((1,), (1,))).astype(LOW)
    grad_gate_two = jnp.sum(own_grad.astype(WIDE) * mlp_rows, axis=0)

    grad_shift_two = jnp.sum(grad_normed_two[0], axis=0)
    grad_scale_two = jnp.sum(grad_normed_two[0] * norm_two[0], axis=0)
    grad_middle = [
        grad_low[k][:own_rows].astype(WIDE)
        + normalize_back(norm_two[k], inverse_two[k], grad_normed_two[k] * (1.0 + scale_two))
        for k in chunks
    ]
    grad_gate_one = jnp.sum(grad_middle[0] * attn_rows[0], axis=0)

    grad_attn = [widen((part * gate_one).astype(LOW)) for part in grad_middle]
    grad_attended = [
        matmul(part, full_out, ((1,), (0,))).astype(LOW).reshape(queries[:chunk_rows].shape)
        for part in grad_attn
    ]
    grad_out = matmul(
        jnp.concatenate(grad_attn, axis=0), jnp.concatenate(attended, axis=0), ((0,), (0,))
    )
    summed_out = scatter_rel(grad_out, "dp", dp)
    parts = [
        attend_back(query_parts[k], key_rows, values, log_totals[k], grad_attended[k])
        for k in chunks
    ]
    grad_queries = jnp.concatenate([part[0] for part in parts], axis=0)
    grad_keys = sum(part[1] for part in parts).astype(LOW)
    grad_values = sum(part[2] for part in parts).astype(LOW)
    grad_projected = jnp.concatenate(
        [part.reshape(length, heads_width) for part in (grad_queries, grad_keys, grad_values)],
        axis=1,
    )
    grad_qkv = matmul(normed_one, grad_projected, ((0,), (0,)))
    grad_qkv, grad_projected = pin(grad_qkv, grad_projected)
    grad_qkv = shrink(grad_qkv, "dp", dp, 0)
    one_terms = [
        matmul(grad_projected[k * chunk_rows : (k + 1) * chunk_rows], full_qkv, ((1,), (1,)))
        for k in chunks
    ]

    grad_mod = jnp.stack(
        [
            sum(jnp.sum(one_terms[k], axis=0) for k in chunks),
            sum(jnp.sum(one_terms[k] * norm_one[k], axis=0) for k in chunks),
            grad_gate_one,
            grad_shift_two,
            grad_scale_two,
            grad_gate_two,
        ]
    )
    grad_mod = sum_all(grad_mod, "tensor", tp).astype(LOW)
    grad_mod, grad_qkv = pin(grad_mod, grad_qkv)
    for bit in range(1, low_bits):
        grad_qkv = shrink(grad_qkv, "dp", dp, bit)
    summed_qkv = jnp.stack(
        [grad_qkv[:, t * heads_width : (t + 1) * heads_width] for t in range(3)], axis=0
    )
    grad_mod = fold_features(grad_mod, "dp", dp)
    summed_ada = jnp.einsum("pkn,pi->kni", grad_mod, signal_all, preferred_element_type=WIDE)
    total = jnp.sum(summed_out * summed_out) + jnp.sum(summed_ada * summed_ada)
    total = total + jnp.sum(summed_up * summed_up) + jnp.sum(summed_down * summed_down)
    total = total + jnp.sum(grad_qkv * grad_qkv)

    one_part = [
        terms[:own_rows] + swap(terms[own_rows:].astype(LOW), 0).astype(WIDE) for terms in one_terms
    ]
    for bit in high_bits:
        one_part = [
            one_part[2 * k] + swap(one_part[2 * k + 1].astype(LOW), bit).astype(WIDE)
            for k in range(len(one_part) // 2)
        ]
    input_grad = grad_middle[0] + normalize_back(
        norm_one[0][:own_rows], inverse_one[0][:own_rows], one_part[0] * (1.0 + scale_one)
    )
    coarse = input_grad.astype(LOW)
    fine = (input_grad - coarse.astype(WIDE)).astype(LOW)
    input_grad = matmul(coarse, select, ((1,), (1,))) + matmul(fine, select, ((1,), (1,)))
    grad_signal = jnp.einsum("pkn,kni->pi", grad_mod, low_ada, preferred_element_type=WIDE)
    for bit in range(low_bits):
        part = grad_signal.shape[0] // 2
        grad_signal = grad_signal[:part] + flip(grad_signal[part:], "dp", dp, bit)
    cond_grad = silu_back(grad_signal)[0]

    total = sum_all(sum_all(total, "tensor", tp), "dp", dp)
    grad_norm = jnp.sqrt(total)
    clip_factor = CLIP_NORM / jnp.maximum(grad_norm, CLIP_NORM)
    qkv = adam_update(qkv_weight, summed_qkv, qkv_moment, qkv_square, clip_factor)
    out = adam_update(out_weight, summed_out, out_moment, out_square, clip_factor)
    up = adam_update(up_weight, summed_up, up_moment, up_square, clip_factor)
    down = adam_update(down_weight, summed_down, down_moment, down_square, clip_factor)
    ada = adam_update(ada_weight, summed_ada, ada_moment, ada_square, clip_factor)
    return (
        block_out[None],
        input_grad[None],
        cond_grad,
        grad_norm,
        *(new for group in zip(qkv, out, up, down, ada) for new in group),
    )


def solution(mesh):
    dp, tp = mesh.shape["dp"], mesh.shape["tensor"]
    rows = P("dp", "tensor", None)
    plain = P("dp", "tensor")
    stacked = P(None, "dp", "tensor")
    weights = (stacked, plain, plain, plain, stacked)

    def step(*arrays):
        return on_device(dp, tp, *arrays)

    return jax.shard_map(
        step,
        mesh=mesh,
        in_specs=(rows, plain, rows) + weights * 3,
        out_specs=(rows, rows, plain, P()) + weights * 3,
        check_vma=False,
    )
```

```python
import jax
import jax.numpy as jnp
import numpy as np
from jax import lax
from jax.experimental import pallas as pl
from jax.experimental.pallas import tpu as pltpu
from jax.sharding import PartitionSpec as P

HEAD_DIM = 72
SCORE_SCALE = HEAD_DIM ** (-0.5)
QUERY_ROWS = 256
STEP = 10

EPS_NORM = 1e-06
CLIP_NORM = 1.0
LEARN_RATE = 0.05
WEIGHT_DECAY = 0.1
BETA_ONE = 0.9
BETA_TWO = 0.999
EPS_ADAM = 1e-08

LOW = jnp.bfloat16
WIDE = jnp.float32


def bit_count(size):
    return size.bit_length() - 1


def flip(value, axis, size, bit):
    return lax.ppermute(value, axis, [(i, i ^ (1 << bit)) for i in range(size)])


def grow(value, axis, size, bit):
    return jnp.concatenate([value, flip(value, axis, size, bit)], axis=0)


def shrink(value, axis, size, bit):
    half = value.shape[0] // 2
    moved = flip(value[half:].astype(LOW), axis, size, bit)
    return value[:half] + moved.astype(WIDE)


def gather_rel(value, axis, size):
    for bit in reversed(range(bit_count(size))):
        value = grow(value, axis, size, bit)
    return value


def scatter_rel(value, axis, size):
    for bit in range(bit_count(size)):
        value = shrink(value, axis, size, bit)
    return value


def spread_features(value, axis, size, bit):
    pairs = value.reshape((value.shape[0] // 2, 2) + value.shape[1:])
    moved = flip(pairs[:, 1], axis, size, bit)
    return jnp.concatenate([pairs[:, 0], moved], axis=-1)


def fold_features(value, axis, size):
    value = value[None]
    for bit in range(bit_count(size)):
        half = value.shape[-1] // 2
        moved = flip(value[..., half:], axis, size, bit)
        value = jnp.stack([value[..., :half], moved], axis=1)
        value = value.reshape((-1,) + value.shape[2:])
    return value


def sum_all(value, axis, size):
    for bit in range(bit_count(size)):
        value = value + flip(value, axis, size, bit)
    return value


def pin(*values):
    return lax.optimization_barrier(values)


def reversed_bits(size):
    bits = bit_count(size)
    return np.array([int(format(i, f"0{bits}b")[::-1], 2) if bits else 0 for i in range(size)])


def selection(index, size, width):
    block = width // size
    place = np.arange(width)
    source = (index ^ jnp.asarray(reversed_bits(size)[place // block], jnp.int32)) * block
    source = source + jnp.asarray(place % block, jnp.int32)
    return (lax.broadcasted_iota(jnp.int32, (width, width), 0) == source[None, :]).astype(LOW)


def matmul(left, right, dims):
    return lax.dot_general(left, right, (dims, ((), ())), preferred_element_type=WIDE)


def normalize(values):
    centre = values - jnp.mean(values, axis=-1, keepdims=True)
    spread = jnp.mean(centre * centre, axis=-1, keepdims=True)
    inverse = lax.rsqrt(spread + EPS_NORM)
    return centre * inverse, inverse


def normalize_back(normed, inverse, grad):
    mean_grad = jnp.mean(grad, axis=-1, keepdims=True)
    mean_both = jnp.mean(grad * normed, axis=-1, keepdims=True)
    return inverse * (grad - mean_grad - normed * mean_both)


def gelu_tanh(values):
    return jax.nn.gelu(values, approximate=True)


def attend_kernel(query_ref, all_ref, out_ref, log_ref):
    heads_width = out_ref.shape[1]
    for head in range(heads_width // HEAD_DIM):
        place = head * HEAD_DIM
        queries = query_ref[:, place : place + HEAD_DIM]
        keys = all_ref[:, heads_width + place : heads_width + place + HEAD_DIM]
        values = all_ref[:, 2 * heads_width + place : 2 * heads_width + place + HEAD_DIM]
        scores = matmul(keys, queries, ((1,), (1,)))
        peak = jnp.max(scores, axis=0, keepdims=True)
        exponent = jnp.exp((scores - peak) * SCORE_SCALE)
        total = jnp.sum(exponent, axis=0, keepdims=True)
        probability = (exponent * (1.0 / total)).astype(LOW)
        mixture = matmul(values, probability, ((0,), (0,)))
        out_ref[:, place : place + HEAD_DIM] = mixture.T.astype(LOW)
        log_ref[head : head + 1, :] = peak * SCORE_SCALE + jnp.log(total)


def attend(projected, chunk, chunk_rows):
    length, all_width = projected.shape
    heads_width = all_width // 3
    rows = min(QUERY_ROWS, chunk_rows)
    start = chunk * chunk_rows // rows
    return pl.pallas_call(
        attend_kernel,
        grid=(chunk_rows // rows,),
        in_specs=[
            pl.BlockSpec((rows, all_width), lambda i: (start + i, 0)),
            pl.BlockSpec((length, all_width), lambda i: (0, 0)),
        ],
        out_specs=[
            pl.BlockSpec((rows, heads_width), lambda i: (i, 0)),
            pl.BlockSpec((heads_width // HEAD_DIM, rows), lambda i: (0, i)),
        ],
        out_shape=[
            jax.ShapeDtypeStruct((chunk_rows, heads_width), LOW),
            jax.ShapeDtypeStruct((heads_width // HEAD_DIM, chunk_rows), WIDE),
        ],
        compiler_params=pltpu.CompilerParams(vmem_limit_bytes=24 << 20),
        cost_estimate=pl.CostEstimate(flops=1, bytes_accessed=1, transcendentals=0),
        name="attend",
    )(projected, projected)


def attend_back_kernel(query_ref, all_ref, log_ref, grad_ref, out_ref, key_sum, value_sum):
    heads_width = grad_ref.shape[1]
    rows = query_ref.shape[0]
    step = pl.program_id(0)

    @pl.when(step == 0)
    def _():
        key_sum[...] = jnp.zeros_like(key_sum)
        value_sum[...] = jnp.zeros_like(value_sum)

    for head in range(heads_width // HEAD_DIM):
        place = head * HEAD_DIM
        queries = query_ref[:, place : place + HEAD_DIM]
        keys = all_ref[:, heads_width + place : heads_width + place + HEAD_DIM]
        values = all_ref[:, 2 * heads_width + place : 2 * heads_width + place + HEAD_DIM]
        grads = grad_ref[:, place : place + HEAD_DIM]
        scores = matmul(keys, queries, ((1,), (1,)))
        probability = jnp.exp(scores * SCORE_SCALE - log_ref[head : head + 1, :])
        grad_probability = matmul(values, grads, ((1,), (1,)))
        inner = jnp.sum(probability * grad_probability, axis=0, keepdims=True)
        grad_scores = (probability * (grad_probability - inner)).astype(LOW)
        key_sum[head] += matmul(grad_scores, queries, ((1,), (0,)))
        value_sum[head] += matmul(probability.astype(LOW), grads, ((1,), (0,)))
        grad_query = matmul(keys, grad_scores, ((0,), (0,))) * SCORE_SCALE
        out_ref[pl.ds(pl.multiple_of(step * rows, rows), rows), place : place + HEAD_DIM] = (
            grad_query.T.astype(LOW)
        )

    @pl.when(step == pl.num_programs(0) - 1)
    def _():
        for head in range(heads_width // HEAD_DIM):
            place = heads_width + head * HEAD_DIM
            out_ref[:, place : place + HEAD_DIM] = (key_sum[head] * SCORE_SCALE).astype(LOW)
            place += heads_width
            out_ref[:, place : place + HEAD_DIM] = value_sum[head].astype(LOW)


def attend_back(projected, log_totals, grad_attended):
    length, all_width = projected.shape
    heads_width = all_width // 3
    heads = heads_width // HEAD_DIM
    rows = min(QUERY_ROWS, length)
    return pl.pallas_call(
        attend_back_kernel,
        grid=(length // rows,),
        in_specs=[
            pl.BlockSpec((rows, all_width), lambda i: (i, 0)),
            pl.BlockSpec((length, all_width), lambda i: (0, 0)),
            pl.BlockSpec((heads, rows), lambda i: (0, i)),
            pl.BlockSpec((rows, heads_width), lambda i: (i, 0)),
        ],
        out_specs=pl.BlockSpec((length, all_width), lambda i: (0, 0)),
        out_shape=jax.ShapeDtypeStruct((length, all_width), LOW),
        scratch_shapes=[
            pltpu.VMEM((heads, length, HEAD_DIM), WIDE),
            pltpu.VMEM((heads, length, HEAD_DIM), WIDE),
        ],
        compiler_params=pltpu.CompilerParams(vmem_limit_bytes=36 << 20),
        cost_estimate=pl.CostEstimate(flops=1, bytes_accessed=1, transcendentals=0),
        name="attend_back",
    )(projected, projected, log_totals, grad_attended)


def token_terms_kernel(grad_ref, weight_ref, norm_ref, terms_ref, sums_ref):
    terms = matmul(grad_ref[...], weight_ref[...], ((1,), (1,)))
    terms_ref[...] = terms

    @pl.when(pl.program_id(0) == 0)
    def _():
        sums_ref[...] = jnp.zeros_like(sums_ref)

    sums_ref[0:1] += jnp.sum(terms, axis=0, keepdims=True)
    sums_ref[1:2] += jnp.sum(terms * norm_ref[...], axis=0, keepdims=True)


def token_terms(grads, weight, normed, chunk):
    chunk_rows, width = normed.shape
    rows = min(QUERY_ROWS, chunk_rows)
    start = chunk * chunk_rows // rows
    return pl.pallas_call(
        token_terms_kernel,
        grid=(chunk_rows // rows,),
        in_specs=[
            pl.BlockSpec((rows, grads.shape[1]), lambda i: (start + i, 0)),
            pl.BlockSpec(weight.shape, lambda i: (0, 0)),
            pl.BlockSpec((rows, width), lambda i: (i, 0)),
        ],
        out_specs=[
            pl.BlockSpec((rows, width), lambda i: (i, 0)),
            pl.BlockSpec((2, width), lambda i: (0, 0)),
        ],
        out_shape=[
            jax.ShapeDtypeStruct((chunk_rows, width), WIDE),
            jax.ShapeDtypeStruct((2, width), WIDE),
        ],
        compiler_params=pltpu.CompilerParams(vmem_limit_bytes=24 << 20),
        cost_estimate=pl.CostEstimate(flops=1, bytes_accessed=1, transcendentals=0),
        name="token_terms",
    )(grads, weight, normed)


def adam_update(weight, gradient, moment, square, clip_factor):
    clipped = gradient * clip_factor
    moment_new = BETA_ONE * moment + (1.0 - BETA_ONE) * clipped
    square_new = BETA_TWO * square + (1.0 - BETA_TWO) * clipped * clipped
    mean_hat = moment_new / (1.0 - BETA_ONE**STEP)
    square_hat = square_new / (1.0 - BETA_TWO**STEP)
    weight_new = weight - LEARN_RATE * (
        mean_hat / (jnp.sqrt(square_hat) + EPS_ADAM) + WEIGHT_DECAY * weight
    )
    return (weight_new, moment_new, square_new)


def on_device(
    dp,
    tp,
    tokens,
    conditioning,
    out_grad,
    qkv_weight,
    out_weight,
    up_weight,
    down_weight,
    ada_weight,
    qkv_moment,
    out_moment,
    up_moment,
    down_moment,
    ada_moment,
    qkv_square,
    out_square,
    up_square,
    down_square,
    ada_square,
):
    width = tokens.shape[-1]
    heads_width = out_weight.shape[-1]
    here = lax.axis_index("dp")
    select = selection(here, dp, width)
    low_bits = bit_count(dp)
    high_bits = range(1, bit_count(tp))
    chunks = range(tp // 2)

    def swap(value, bit):
        return flip(value, "tensor", tp, bit)

    def widen(value):
        return jnp.concatenate([value, swap(value, 0)], axis=0)

    def all_blocks(value):
        pieces = [value]
        for bit in reversed(high_bits):
            pieces = pieces + [swap(piece, bit) for piece in pieces]
        return pieces

    def token_sum(kept, sent):
        return high_sum([keep + swap(send, 0).astype(WIDE) for keep, send in zip(kept, sent)])

    def high_sum(part):
        for bit in high_bits:
            low_part = [value.astype(LOW) for value in part]
            moved = [swap(value, bit) for value in low_part]
            part = [
                low_part[k].astype(WIDE) + moved[k ^ (1 << (bit - 1))].astype(WIDE) for k in chunks
            ]
        return part

    def split_product(left, right, dims):
        rows = left.shape[0] // 2
        return pin(matmul(left[:rows], right, dims), matmul(left[rows:], right, dims).astype(LOW))

    signal, silu_back = jax.vjp(jax.nn.silu, conditioning)
    low_ada = ada_weight.astype(LOW)
    high, middle_bits = low_bits - 1, list(reversed(range(1, low_bits - 1)))

    def grow_all(value, bits):
        for bit in bits:
            value = grow(value, "dp", dp, bit)
        return value

    signal_all = grow(signal.astype(LOW), "dp", dp, high)
    full_qkv = jnp.concatenate([qkv_weight[t].astype(LOW) for t in range(3)], axis=1)
    signal_all, full_qkv = pin(signal_all, full_qkv)
    full_qkv = grow(full_qkv, "dp", dp, high)
    own_tokens = matmul(tokens[0], select, ((1,), (0,))).astype(LOW)
    own_grad = matmul(out_grad[0], select, ((1,), (0,))).astype(LOW)
    signal_all = grow_all(signal_all, middle_bits + [0])
    tokens_low = all_blocks(own_tokens)
    modulation = jnp.einsum("pi,kni->pkn", signal_all, low_ada, preferred_element_type=WIDE)
    modulation, full_qkv = pin(modulation, full_qkv)
    modulation = sum_all(modulation, "tensor", tp)
    for bit in [high] + middle_bits:
        modulation = spread_features(modulation, "dp", dp, bit)
    modulation, full_qkv, tokens_low, own_grad = pin(modulation, full_qkv, tokens_low, own_grad)
    full_qkv = grow_all(full_qkv, middle_bits)
    tokens_low = [widen(piece) for piece in tokens_low]
    modulation = spread_features(modulation, "dp", dp, 0)
    modulation = modulation.reshape(6, 1, width)
    shift_one, scale_one, gate_one, shift_two, scale_two, gate_two = modulation

    tokens_wide = [value.astype(WIDE) for value in tokens_low]
    norm_one, inverse_one = zip(*(pin(*normalize(value)) for value in tokens_wide))
    normed_one = [(value * (1.0 + scale_one) + shift_one).astype(LOW) for value in norm_one]
    normed_one = jnp.concatenate(normed_one, axis=0)
    lows = [weight.astype(LOW) for weight in (out_weight, up_weight, down_weight)]
    normed_one, full_qkv, (full_out, full_up, full_down) = pin(normed_one, full_qkv, lows)
    full_qkv = grow(full_qkv, "dp", dp, 0)
    full_out = grow(full_out, "dp", dp, high)
    full_out, full_up = pin(full_out, full_up)
    full_out = grow_all(full_out, middle_bits)
    full_up = grow(full_up, "dp", dp, high)
    full_qkv, full_out, full_up, full_down = pin(full_qkv, full_out, full_up, full_down)
    full_out = grow(full_out, "dp", dp, 0)
    full_up = grow_all(full_up, middle_bits[:-1] + [0])
    full_down = grow(full_down, "dp", dp, high)
    projected = matmul(normed_one, full_qkv, ((1,), (0,))).astype(LOW)
    length = projected.shape[0]
    chunk_rows = length // len(chunks)
    attended, log_totals = map(list, zip(*(attend(projected, k, chunk_rows) for k in chunks)))
    attended[0], full_out, full_up, full_down = pin(attended[0], full_out, full_up, full_down)
    full_down = grow_all(full_down, middle_bits)
    attn_terms = zip(*(split_product(part, full_out, ((1,), (1,))) for part in attended))
    part = [keep + swap(send, 0).astype(WIDE) for keep, send in zip(*attn_terms)]
    part, full_down, full_up, own_grad = pin(part, full_down, full_up, own_grad)
    attn_rows = high_sum(part)
    grad_low = [widen(piece) for piece in all_blocks(own_grad)]
    own_rows = attn_rows[0].shape[0]
    middle = [tokens_wide[k][:own_rows] + gate_one * attn_rows[k] for k in chunks]
    norm_two, inverse_two = zip(*(normalize(value) for value in middle))
    normed_two = [(value * (1.0 + scale_two) + shift_two).astype(LOW) for value in norm_two]
    seq_two = [widen(value) for value in normed_two]
    moved = flip(full_up, "dp", dp, middle_bits[-1])
    part = moved.shape[0] // 2
    full_up = jnp.concatenate([full_up[:part], moved[:part], full_up[part:], moved[part:]], axis=0)
    full_down = grow(full_down, "dp", dp, 0)

    pre_act = [matmul(part, full_up, ((1,), (0,))) for part in seq_two]
    activated, gelu_back = zip(*(jax.vjp(gelu_tanh, part) for part in pre_act))
    hidden = [part.astype(LOW) for part in activated]

    grad_mlp = [(part.astype(WIDE) * gate_two).astype(LOW) for part in grad_low]
    grad_hidden = [matmul(part, full_down, ((1,), (0,))) for part in grad_mlp]
    grad_pre = [back(part)[0].astype(LOW) for back, part in zip(gelu_back, grad_hidden)]
    grad_terms = zip(*(split_product(part, full_up, ((1,), (1,))) for part in grad_pre))
    grad_normed_two = token_sum(*grad_terms)
    all_hidden = jnp.concatenate(hidden, axis=0)
    grad_down = matmul(jnp.concatenate(grad_mlp, axis=0), all_hidden, ((0,), (0,)))
    summed_down = scatter_rel(grad_down, "dp", dp)
    all_seq_two = jnp.concatenate(seq_two, axis=0)
    grad_up = matmul(all_seq_two, jnp.concatenate(grad_pre, axis=0), ((0,), (0,)))
    summed_up = scatter_rel(grad_up, "dp", dp)

    mlp_kept, mlp_sent = zip(*(split_product(part, full_down, ((1,), (1,))) for part in hidden))
    mlp_part = [keep + swap(send, 0).astype(WIDE) for keep, send in zip(mlp_kept, mlp_sent)]
    for bit in high_bits:
        mlp_part = [
            mlp_part[2 * k] + swap(mlp_part[2 * k + 1].astype(LOW), bit).astype(WIDE)
            for k in range(len(mlp_part) // 2)
        ]
    mlp_rows = mlp_part[0]
    block_out = (middle[0] + gate_two * mlp_rows).astype(LOW)
    block_out = matmul(block_out, select, ((1,), (1,))).astype(LOW)
    grad_gate_two = jnp.sum(own_grad.astype(WIDE) * mlp_rows, axis=0)

    grad_shift_two = jnp.sum(grad_normed_two[0], axis=0)
    grad_scale_two = jnp.sum(grad_normed_two[0] * norm_two[0], axis=0)
    grad_middle = [
        grad_low[k][:own_rows].astype(WIDE)
        + normalize_back(norm_two[k], inverse_two[k], grad_normed_two[k] * (1.0 + scale_two))
        for k in chunks
    ]
    grad_gate_one = jnp.sum(grad_middle[0] * attn_rows[0], axis=0)

    grad_attn = [widen((part * gate_one).astype(LOW)) for part in grad_middle]
    grad_attended = [
        matmul(part, full_out, ((1,), (0,))).astype(LOW)
        for part in grad_attn
    ]
    grad_out = matmul(
        jnp.concatenate(grad_attn, axis=0), jnp.concatenate(attended, axis=0), ((0,), (0,))
    )
    split = width // 2
    kept_out, sent_out, grad_attended = pin(
        grad_out[:split], grad_out[split:].astype(LOW), grad_attended
    )
    sent_out = flip(sent_out, "dp", dp, 0)
    grad_projected = attend_back(
        projected, jnp.concatenate(log_totals, axis=1), jnp.concatenate(grad_attended, axis=0)
    )
    sent_out, grad_projected = pin(sent_out, grad_projected)
    grad_out = kept_out + sent_out.astype(WIDE)
    grad_qkv = matmul(normed_one, grad_projected, ((0,), (0,)))
    kept_qkv, sent_qkv, grad_projected = pin(
        grad_qkv[:split], grad_qkv[split:].astype(LOW), grad_projected
    )
    sent_qkv = flip(sent_qkv, "dp", dp, 0)
    one_terms, one_sums = zip(
        *(token_terms(grad_projected, full_qkv, norm_one[k], k) for k in chunks)
    )
    one_terms, one_sums, sent_qkv = pin(one_terms, one_sums, sent_qkv)
    grad_qkv = kept_qkv + sent_qkv.astype(WIDE)

    for bit in range(1, low_bits - 1):
        grad_qkv = shrink(grad_qkv, "dp", dp, bit)
    rest = jnp.stack([grad_gate_one, grad_shift_two, grad_scale_two, grad_gate_two])
    grad_mod = jnp.concatenate([sum(one_sums), rest], axis=0)
    grad_mod = grad_mod + swap(grad_mod, 0)
    one_part = [
        terms[:own_rows] + swap(terms[own_rows:].astype(LOW), 0).astype(WIDE) for terms in one_terms
    ]
    for bit in high_bits:
        grad_mod = grad_mod + swap(grad_mod, bit)
    grad_mod, grad_qkv, one_part, grad_out = pin(
        grad_mod.astype(LOW), grad_qkv, one_part, grad_out
    )
    grad_qkv = shrink(grad_qkv, "dp", dp, high)
    for bit in high_bits:
        one_part = [
            one_part[2 * k] + swap(one_part[2 * k + 1].astype(LOW), bit).astype(WIDE)
            for k in range(len(one_part) // 2)
        ]
    grad_mod = fold_features(grad_mod, "dp", dp)
    for bit in range(1, low_bits - 1):
        grad_out = shrink(grad_out, "dp", dp, bit)
    grad_mod, grad_qkv, grad_out, one_part = pin(grad_mod, grad_qkv, grad_out, one_part)
    summed_out = shrink(grad_out, "dp", dp, high)
    summed_ada = jnp.einsum("pkn,pi->kni", grad_mod, signal_all, preferred_element_type=WIDE)
    summed_qkv = jnp.stack(
        [grad_qkv[:, t * heads_width : (t + 1) * heads_width] for t in range(3)], axis=0
    )
    total = jnp.sum(grad_qkv * grad_qkv) + jnp.sum(summed_ada * summed_ada)
    total = total + jnp.sum(summed_up * summed_up) + jnp.sum(summed_down * summed_down)
    total = total + jnp.sum(summed_out * summed_out)

    input_grad = grad_middle[0] + normalize_back(
        norm_one[0][:own_rows], inverse_one[0][:own_rows], one_part[0] * (1.0 + scale_one)
    )
    coarse = input_grad.astype(LOW)
    fine = (input_grad - coarse.astype(WIDE)).astype(LOW)
    input_grad = matmul(coarse, select, ((1,), (1,))) + matmul(fine, select, ((1,), (1,)))
    grad_signal = jnp.einsum("pkn,kni->pi", grad_mod, low_ada, preferred_element_type=WIDE)
    for bit in range(low_bits):
        part = grad_signal.shape[0] // 2
        grad_signal = grad_signal[:part] + flip(grad_signal[part:], "dp", dp, bit)
    cond_grad = silu_back(grad_signal)[0]

    total = sum_all(total, "tensor", tp)
    total, input_grad, block_out, cond_grad = pin(total, input_grad, block_out, cond_grad)
    total = sum_all(total, "dp", dp)
    grad_norm = jnp.sqrt(total)
    clip_factor = CLIP_NORM / jnp.maximum(grad_norm, CLIP_NORM)
    qkv = adam_update(qkv_weight, summed_qkv, qkv_moment, qkv_square, clip_factor)
    out = adam_update(out_weight, summed_out, out_moment, out_square, clip_factor)
    up = adam_update(up_weight, summed_up, up_moment, up_square, clip_factor)
    down = adam_update(down_weight, summed_down, down_moment, down_square, clip_factor)
    ada = adam_update(ada_weight, summed_ada, ada_moment, ada_square, clip_factor)
    return (
        block_out[None],
        input_grad[None],
        cond_grad,
        grad_norm,
        *(new for group in zip(qkv, out, up, down, ada) for new in group),
    )


def solution(mesh):
    dp, tp = mesh.shape["dp"], mesh.shape["tensor"]
    rows = P("dp", "tensor", None)
    plain = P("dp", "tensor")
    stacked = P(None, "dp", "tensor")
    weights = (stacked, plain, plain, plain, stacked)

    def step(*arrays):
        return on_device(dp, tp, *arrays)

    return jax.shard_map(
        step,
        mesh=mesh,
        in_specs=(rows, plain, rows) + weights * 3,
        out_specs=(rows, rows, plain, P()) + weights * 3,
        check_vma=False,
    )
```

```python
import functools

import jax
import jax.numpy as jnp
import numpy as np
from jax import lax
from jax.experimental import pallas as pl
from jax.experimental.pallas import tpu as pltpu
from jax.sharding import PartitionSpec as P

HEAD_DIM = 72
SCORE_SCALE = HEAD_DIM ** (-0.5)
QUERY_ROWS = 256
COLUMN_BLOCK = 384
STEP = 10

EPS_NORM = 1e-06
CLIP_NORM = 1.0
LEARN_RATE = 0.05
WEIGHT_DECAY = 0.1
BETA_ONE = 0.9
BETA_TWO = 0.999
EPS_ADAM = 1e-08

LOW = jnp.bfloat16
WIDE = jnp.float32


def bit_count(size):
    return size.bit_length() - 1


def flip(value, axis, size, bit):
    return lax.ppermute(value, axis, [(i, i ^ (1 << bit)) for i in range(size)])


def grow(value, axis, size, bit):
    return jnp.concatenate([value, flip(value, axis, size, bit)], axis=0)


def shrink(value, axis, size, bit):
    half = value.shape[0] // 2
    moved = flip(value[half:].astype(LOW), axis, size, bit)
    return value[:half] + moved.astype(WIDE)


def gather_rel(value, axis, size):
    for bit in reversed(range(bit_count(size))):
        value = grow(value, axis, size, bit)
    return value


def scatter_rel(value, axis, size):
    for bit in range(bit_count(size)):
        value = shrink(value, axis, size, bit)
    return value


def spread_features(value, axis, size, bit):
    pairs = value.reshape((value.shape[0] // 2, 2) + value.shape[1:])
    moved = flip(pairs[:, 1], axis, size, bit)
    return jnp.concatenate([pairs[:, 0], moved], axis=-1)


def fold_features(value, axis, size, bits):
    if value.ndim == 2:
        value = value[None]
    for bit in bits:
        half = value.shape[-1] // 2
        moved = flip(value[..., half:], axis, size, bit)
        value = jnp.stack([value[..., :half], moved], axis=1)
        value = value.reshape((-1,) + value.shape[2:])
    return value


def sum_all(value, axis, size):
    for bit in range(bit_count(size)):
        value = value + flip(value, axis, size, bit)
    return value


def pin(*values):
    return lax.optimization_barrier(values)


def reversed_bits(size):
    bits = bit_count(size)
    return np.array([int(format(i, f"0{bits}b")[::-1], 2) if bits else 0 for i in range(size)])


def selection(index, size, width):
    block = width // size
    place = np.arange(width)
    source = (index ^ jnp.asarray(reversed_bits(size)[place // block], jnp.int32)) * block
    source = source + jnp.asarray(place % block, jnp.int32)
    return (lax.broadcasted_iota(jnp.int32, (width, width), 0) == source[None, :]).astype(LOW)


def matmul(left, right, dims):
    return lax.dot_general(left, right, (dims, ((), ())), preferred_element_type=WIDE)


def normalize(values):
    centre = values - jnp.mean(values, axis=-1, keepdims=True)
    spread = jnp.mean(centre * centre, axis=-1, keepdims=True)
    inverse = lax.rsqrt(spread + EPS_NORM)
    return centre * inverse, inverse


def normalize_back(normed, inverse, grad):
    mean_grad = jnp.mean(grad, axis=-1, keepdims=True)
    mean_both = jnp.mean(grad * normed, axis=-1, keepdims=True)
    return inverse * (grad - mean_grad - normed * mean_both)


def gelu_tanh(values):
    return jax.nn.gelu(values, approximate=True)


def work(flops, weight):
    return pl.CostEstimate(flops=weight * flops, bytes_accessed=1 << 20, transcendentals=0)


def attend_kernel(query_ref, all_ref, out_ref, log_ref):
    heads_width = out_ref.shape[1]
    for head in range(heads_width // HEAD_DIM):
        place = head * HEAD_DIM
        queries = query_ref[:, place : place + HEAD_DIM]
        keys = all_ref[:, heads_width + place : heads_width + place + HEAD_DIM]
        values = all_ref[:, 2 * heads_width + place : 2 * heads_width + place + HEAD_DIM]
        scores = matmul(keys, queries, ((1,), (1,)))
        peak = jnp.max(scores, axis=0, keepdims=True)
        exponent = jnp.exp((scores - peak) * SCORE_SCALE)
        total = jnp.sum(exponent, axis=0, keepdims=True)
        probability = (exponent * (1.0 / total)).astype(LOW)
        mixture = matmul(values, probability, ((0,), (0,)))
        out_ref[:, place : place + HEAD_DIM] = mixture.T.astype(LOW)
        log_ref[head : head + 1, :] = peak * SCORE_SCALE + jnp.log(total)


def attend(projected, chunk, chunk_rows):
    length, all_width = projected.shape
    heads_width = all_width // 3
    rows = min(QUERY_ROWS, chunk_rows)
    start = chunk * chunk_rows // rows
    return pl.pallas_call(
        attend_kernel,
        grid=(chunk_rows // rows,),
        in_specs=[
            pl.BlockSpec((rows, all_width), lambda i: (start + i, 0)),
            pl.BlockSpec((length, all_width), lambda i: (0, 0)),
        ],
        out_specs=[
            pl.BlockSpec((rows, heads_width), lambda i: (i, 0)),
            pl.BlockSpec((heads_width // HEAD_DIM, rows), lambda i: (0, i)),
        ],
        out_shape=[
            jax.ShapeDtypeStruct((chunk_rows, heads_width), LOW),
            jax.ShapeDtypeStruct((heads_width // HEAD_DIM, chunk_rows), WIDE),
        ],
        compiler_params=pltpu.CompilerParams(vmem_limit_bytes=24 << 20),
        cost_estimate=work(4 * chunk_rows * length * heads_width, 4),
        name="attend",
    )(projected, projected)


def attend_back_kernel(query_ref, all_ref, log_ref, grad_ref, out_ref, key_sum, value_sum):
    heads_width = grad_ref.shape[1]
    rows = query_ref.shape[0]
    step = pl.program_id(0)

    @pl.when(step == 0)
    def _():
        key_sum[...] = jnp.zeros_like(key_sum)
        value_sum[...] = jnp.zeros_like(value_sum)

    for head in range(heads_width // HEAD_DIM):
        place = head * HEAD_DIM
        queries = query_ref[:, place : place + HEAD_DIM]
        keys = all_ref[:, heads_width + place : heads_width + place + HEAD_DIM]
        values = all_ref[:, 2 * heads_width + place : 2 * heads_width + place + HEAD_DIM]
        grads = grad_ref[:, place : place + HEAD_DIM]
        scores = matmul(keys, queries, ((1,), (1,)))
        probability = jnp.exp(scores * SCORE_SCALE - log_ref[head : head + 1, :])
        grad_probability = matmul(values, grads, ((1,), (1,)))
        inner = jnp.sum(probability * grad_probability, axis=0, keepdims=True)
        grad_scores = (probability * (grad_probability - inner)).astype(LOW)
        key_sum[head] += matmul(grad_scores, queries, ((1,), (0,)))
        value_sum[head] += matmul(probability.astype(LOW), grads, ((1,), (0,)))
        grad_query = matmul(keys, grad_scores, ((0,), (0,))) * SCORE_SCALE
        out_ref[pl.ds(pl.multiple_of(step * rows, rows), rows), place : place + HEAD_DIM] = (
            grad_query.T.astype(LOW)
        )

    @pl.when(step == pl.num_programs(0) - 1)
    def _():
        for head in range(heads_width // HEAD_DIM):
            place = heads_width + head * HEAD_DIM
            out_ref[:, place : place + HEAD_DIM] = (key_sum[head] * SCORE_SCALE).astype(LOW)
            place += heads_width
            out_ref[:, place : place + HEAD_DIM] = value_sum[head].astype(LOW)


def attend_back(projected, log_totals, grad_attended):
    length, all_width = projected.shape
    heads_width = all_width // 3
    heads = heads_width // HEAD_DIM
    rows = min(QUERY_ROWS, length)
    return pl.pallas_call(
        attend_back_kernel,
        grid=(length // rows,),
        in_specs=[
            pl.BlockSpec((rows, all_width), lambda i: (i, 0)),
            pl.BlockSpec((length, all_width), lambda i: (0, 0)),
            pl.BlockSpec((heads, rows), lambda i: (0, i)),
            pl.BlockSpec((rows, heads_width), lambda i: (i, 0)),
        ],
        out_specs=pl.BlockSpec((length, all_width), lambda i: (0, 0)),
        out_shape=jax.ShapeDtypeStruct((length, all_width), LOW),
        scratch_shapes=[
            pltpu.VMEM((heads, length, HEAD_DIM), WIDE),
            pltpu.VMEM((heads, length, HEAD_DIM), WIDE),
        ],
        compiler_params=pltpu.CompilerParams(vmem_limit_bytes=36 << 20),
        cost_estimate=work(10 * length * length * heads_width, 2),
        name="attend_back",
    )(projected, projected, log_totals, grad_attended)


def token_terms_kernel(grad_ref, weight_ref, norm_ref, terms_ref, sums_ref):
    terms = matmul(grad_ref[...], weight_ref[...], ((1,), (1,)))
    terms_ref[...] = terms

    @pl.when(pl.program_id(0) == 0)
    def _():
        sums_ref[...] = jnp.zeros_like(sums_ref)

    sums_ref[0:1] += jnp.sum(terms, axis=0, keepdims=True)
    sums_ref[1:2] += jnp.sum(terms * norm_ref[...], axis=0, keepdims=True)


def token_terms(grads, weight, normed, chunk):
    chunk_rows, width = normed.shape
    rows = min(QUERY_ROWS, chunk_rows)
    start = chunk * chunk_rows // rows
    return pl.pallas_call(
        token_terms_kernel,
        grid=(chunk_rows // rows,),
        in_specs=[
            pl.BlockSpec((rows, grads.shape[1]), lambda i: (start + i, 0)),
            pl.BlockSpec(weight.shape, lambda i: (0, 0)),
            pl.BlockSpec((rows, width), lambda i: (i, 0)),
        ],
        out_specs=[
            pl.BlockSpec((rows, width), lambda i: (i, 0)),
            pl.BlockSpec((2, width), lambda i: (0, 0)),
        ],
        out_shape=[
            jax.ShapeDtypeStruct((chunk_rows, width), WIDE),
            jax.ShapeDtypeStruct((2, width), WIDE),
        ],
        compiler_params=pltpu.CompilerParams(vmem_limit_bytes=24 << 20),
        cost_estimate=work(2 * chunk_rows * width * grads.shape[1], 1),
        name="token_terms",
    )(grads, weight, normed)


def weight_grad_kernel(pairs, *refs):
    parts = (len(refs) - 2) // 2
    lefts, rights, (kept_ref, sent_ref) = refs[:parts], refs[parts:-2], refs[-2:]
    split, columns = kept_ref.shape
    turned = [left[...].T for left in lefts]
    for start in range(0, columns, COLUMN_BLOCK):
        stop = min(start + COLUMN_BLOCK, columns)
        total = sum(
            matmul(left, right[:, start:stop], ((1,), (0,))) for left, right in zip(turned, rights)
        )
        rows = split // pairs
        for k in range(pairs):
            place = slice(k * rows, (k + 1) * rows)
            kept_ref[place, start:stop] = total[2 * k * rows : (2 * k + 1) * rows]
            sent_ref[place, start:stop] = total[(2 * k + 1) * rows : (2 * k + 2) * rows].astype(LOW)


def weight_grad(lefts, rights, pairs=1):
    split, columns = lefts[0].shape[1] // 2, rights[0].shape[1]
    return pl.pallas_call(
        functools.partial(weight_grad_kernel, pairs),
        out_shape=[
            jax.ShapeDtypeStruct((split, columns), WIDE),
            jax.ShapeDtypeStruct((split, columns), LOW),
        ],
        compiler_params=pltpu.CompilerParams(vmem_limit_bytes=40 << 20),
        cost_estimate=work(4 * sum(left.shape[0] for left in lefts) * split * columns, 1),
        name="weight_grad",
    )(*lefts, *rights)


def adam_update(weight, gradient, moment, square, clip_factor):
    clipped = gradient * clip_factor
    moment_new = BETA_ONE * moment + (1.0 - BETA_ONE) * clipped
    square_new = BETA_TWO * square + (1.0 - BETA_TWO) * clipped * clipped
    mean_hat = moment_new / (1.0 - BETA_ONE**STEP)
    square_hat = square_new / (1.0 - BETA_TWO**STEP)
    weight_new = weight - LEARN_RATE * (
        mean_hat / (jnp.sqrt(square_hat) + EPS_ADAM) + WEIGHT_DECAY * weight
    )
    return (weight_new, moment_new, square_new)


def on_device(
    dp,
    tp,
    tokens,
    conditioning,
    out_grad,
    qkv_weight,
    out_weight,
    up_weight,
    down_weight,
    ada_weight,
    qkv_moment,
    out_moment,
    up_moment,
    down_moment,
    ada_moment,
    qkv_square,
    out_square,
    up_square,
    down_square,
    ada_square,
):
    width = tokens.shape[-1]
    heads_width = out_weight.shape[-1]
    here = lax.axis_index("dp")
    select = selection(here, dp, width)
    low_bits = bit_count(dp)
    high_bits = range(1, bit_count(tp))
    chunks = range(tp // 2)

    def swap(value, bit):
        return flip(value, "tensor", tp, bit)

    def widen(value):
        return jnp.concatenate([value, swap(value, 0)], axis=0)

    def all_blocks(value):
        pieces = [value]
        for bit in reversed(high_bits):
            pieces = pieces + [swap(piece, bit) for piece in pieces]
        return pieces

    def token_sum(kept, sent):
        return high_sum([keep + swap(send, 0).astype(WIDE) for keep, send in zip(kept, sent)])

    def high_sum(part):
        for bit in high_bits:
            low_part = [value.astype(LOW) for value in part]
            moved = [swap(value, bit) for value in low_part]
            part = [
                low_part[k].astype(WIDE) + moved[k ^ (1 << (bit - 1))].astype(WIDE) for k in chunks
            ]
        return part

    def split_product(left, right, dims):
        rows = left.shape[0] // 2
        return pin(matmul(left[:rows], right, dims), matmul(left[rows:], right, dims).astype(LOW))

    signal, silu_back = jax.vjp(jax.nn.silu, conditioning)
    low_ada = ada_weight.astype(LOW)
    high, middle_bits = low_bits - 1, list(reversed(range(1, low_bits - 1)))

    def grow_all(value, bits):
        for bit in bits:
            value = grow(value, "dp", dp, bit)
        return value

    signal_all = grow(signal.astype(LOW), "dp", dp, high)
    full_qkv = jnp.concatenate([qkv_weight[t].astype(LOW) for t in range(3)], axis=1)
    signal_all, full_qkv = pin(signal_all, full_qkv)
    full_qkv = grow(full_qkv, "dp", dp, high)
    own_tokens = matmul(tokens[0], select, ((1,), (0,))).astype(LOW)
    own_grad = matmul(out_grad[0], select, ((1,), (0,))).astype(LOW)
    signal_all = grow_all(signal_all, middle_bits + [0])
    tokens_low = all_blocks(own_tokens)
    modulation = jnp.einsum("pi,kni->pkn", signal_all, low_ada, preferred_element_type=WIDE)
    modulation, full_qkv = pin(modulation, full_qkv)
    full_qkv = grow_all(full_qkv, middle_bits)
    modulation = sum_all(modulation, "tensor", tp)
    count = modulation.shape[0] // 2
    moved = flip(modulation[count:], "dp", dp, 0)
    modulation = jnp.concatenate([modulation[:count], moved], axis=-1)
    modulation, full_qkv, tokens_low, own_grad = pin(modulation, full_qkv, tokens_low, own_grad)
    full_qkv = grow(full_qkv, "dp", dp, 0)
    tokens_low = [widen(piece) for piece in tokens_low]
    for bit in [high] + middle_bits:
        modulation = spread_features(modulation, "dp", dp, bit)
    piece = width // dp
    modulation = jnp.concatenate(
        [
            modulation[0, :, (2 * k + low_bit) * piece : (2 * k + low_bit + 1) * piece]
            for low_bit in range(2)
            for k in range(dp // 2)
        ],
        axis=-1,
    )
    modulation = modulation.reshape(6, 1, width)
    shift_one, scale_one, gate_one, shift_two, scale_two, gate_two = modulation

    tokens_wide = [value.astype(WIDE) for value in tokens_low]
    norm_one, inverse_one = zip(*(pin(*normalize(value)) for value in tokens_wide))
    normed_one = [(value * (1.0 + scale_one) + shift_one).astype(LOW) for value in norm_one]
    normed_one = jnp.concatenate(normed_one, axis=0)
    lows = [weight.astype(LOW) for weight in (out_weight, up_weight, down_weight)]
    normed_one, own_grad, (full_out, full_up, full_down) = pin(normed_one, own_grad, lows)
    grad_low = all_blocks(own_grad)
    full_out = grow(full_out, "dp", dp, high)
    full_out, full_up = pin(full_out, full_up)
    full_out = grow_all(full_out, middle_bits)
    full_up = grow(full_up, "dp", dp, high)
    full_qkv, full_out, full_down = pin(full_qkv, full_out, full_down)
    full_out = grow(full_out, "dp", dp, 0)
    full_down = grow(full_down, "dp", dp, high)
    projected = matmul(normed_one, full_qkv, ((1,), (0,))).astype(LOW)
    length = projected.shape[0]
    chunk_rows = length // len(chunks)
    attended, log_totals, part = [], [], []
    for k in chunks:
        mixed, log_total = attend(projected, k, chunk_rows)
        if k == 0:
            mixed, full_out, full_up, grad_low = pin(mixed, full_out, full_up, grad_low)
            full_up = grow_all(full_up, middle_bits[:-1] + [0])
        keep, send = split_product(mixed, full_out, ((1,), (1,)))
        part.append(keep + swap(send, 0).astype(WIDE))
        part[k], projected = pin(part[k], projected)
        attended.append(mixed)
        log_totals.append(log_total)
    part, full_up, full_down = pin(part, full_up, full_down)
    full_down = grow_all(full_down, middle_bits)
    attn_rows = high_sum(part)
    attn_rows[0], full_down, full_up = pin(attn_rows[0], full_down, full_up)
    moved_up = flip(full_up, "dp", dp, middle_bits[-1])
    moved_down = flip(full_down, "dp", dp, 0)
    attn_rows, moved_up, moved_down, grad_low = pin(attn_rows, moved_up, moved_down, grad_low)
    grad_low = [widen(piece) for piece in grad_low]
    own_rows = attn_rows[0].shape[0]
    middle = [tokens_wide[k][:own_rows] + gate_one * attn_rows[k] for k in chunks]
    norm_two, inverse_two = zip(*(normalize(value) for value in middle))
    normed_two = [(value * (1.0 + scale_two) + shift_two).astype(LOW) for value in norm_two]
    seq_two = [widen(value) for value in normed_two]
    rows = full_up.shape[0] // 2
    full_up = jnp.concatenate(
        [full_up[:rows], moved_up[:rows], full_up[rows:], moved_up[rows:]], axis=0
    )
    full_down = jnp.concatenate([full_down, moved_down], axis=0)

    pre_act = [matmul(part, full_up, ((1,), (0,))) for part in seq_two]
    activated, gelu_back = zip(*(jax.vjp(gelu_tanh, part) for part in pre_act))
    hidden = [part.astype(LOW) for part in activated]

    grad_mlp = [(part.astype(WIDE) * gate_two).astype(LOW) for part in grad_low]
    kept_down, sent_down = weight_grad(grad_mlp, hidden)
    kept_down, sent_down, grad_mlp, hidden = pin(kept_down, sent_down, grad_mlp, hidden)
    sent_down = flip(sent_down, "dp", dp, 0)
    grad_hidden = [matmul(part, full_down, ((1,), (0,))) for part in grad_mlp]
    grad_pre = [back(part)[0].astype(LOW) for back, part in zip(gelu_back, grad_hidden)]
    part = []
    for k in chunks:
        keep, send = split_product(grad_pre[k], full_up, ((1,), (1,)))
        part.append(keep + swap(send, 0).astype(WIDE))
    part, grad_pre, seq_two = pin(part, grad_pre, seq_two)
    kept_up, sent_up = weight_grad(seq_two, grad_pre, 2)
    grad_normed_two = high_sum(part)
    grad_normed_two[0], kept_up, sent_up, sent_down = pin(
        grad_normed_two[0], kept_up, sent_up, sent_down
    )
    grad_down = kept_down + sent_down.astype(WIDE)
    for bit in range(1, low_bits - 1):
        grad_down = shrink(grad_down, "dp", dp, bit)

    grad_shift_two = jnp.sum(grad_normed_two[0], axis=0)
    grad_scale_two = jnp.sum(grad_normed_two[0] * norm_two[0], axis=0)
    grad_middle = [
        grad_low[k][:own_rows].astype(WIDE)
        + normalize_back(norm_two[k], inverse_two[k], grad_normed_two[k] * (1.0 + scale_two))
        for k in chunks
    ]
    grad_gate_one = jnp.sum(grad_middle[0] * attn_rows[0], axis=0)

    grad_attn = [widen((part * gate_one).astype(LOW)) for part in grad_middle]
    grad_attended = [
        matmul(part, full_out, ((1,), (0,))).astype(LOW)
        for part in grad_attn
    ]
    kept_out, sent_out = weight_grad(grad_attn, attended)
    kept_out, sent_out, grad_attended = pin(kept_out, sent_out, grad_attended)
    sent_up = flip(sent_up, "dp", dp, 1)
    sent_out = flip(sent_out, "dp", dp, 0)
    grad_projected = attend_back(
        projected, jnp.concatenate(log_totals, axis=1), jnp.concatenate(grad_attended, axis=0)
    )

    grad_projected, sent_out = pin(grad_projected, sent_out)
    grad_out = kept_out + sent_out.astype(WIDE)
    for bit in range(1, low_bits - 1):
        grad_out = shrink(grad_out, "dp", dp, bit)
    kept_qkv, sent_qkv = weight_grad([normed_one], [grad_projected])
    kept_qkv, sent_qkv, grad_projected, hidden = pin(kept_qkv, sent_qkv, grad_projected, hidden)
    sent_qkv = flip(sent_qkv, "dp", dp, 0)
    mlp_kept, mlp_sent = zip(*(split_product(part, full_down, ((1,), (1,))) for part in hidden))
    mlp_part = [keep + swap(send, 0).astype(WIDE) for keep, send in zip(mlp_kept, mlp_sent)]
    mlp_part, grad_projected = pin(mlp_part, grad_projected)
    for bit in high_bits:
        mlp_part = [
            mlp_part[2 * k] + swap(mlp_part[2 * k + 1].astype(LOW), bit).astype(WIDE)
            for k in range(len(mlp_part) // 2)
        ]
    mlp_rows = mlp_part[0]
    block_out = (middle[0] + gate_two * mlp_rows).astype(LOW)
    block_out = matmul(block_out, select, ((1,), (1,))).astype(LOW)
    grad_gate_two = jnp.sum(own_grad.astype(WIDE) * mlp_rows, axis=0)
    one_terms, one_sums = zip(
        *(token_terms(grad_projected, full_qkv, norm_one[k], k) for k in chunks)
    )
    rest = jnp.stack([grad_gate_one, grad_shift_two, grad_scale_two, grad_gate_two])
    one_sums, one_terms, sent_qkv, grad_out, rest, sent_up, grad_down = pin(
        one_sums, one_terms, sent_qkv, grad_out, rest, sent_up, grad_down
    )
    grad_up = kept_up + sent_up.astype(WIDE)
    grad_up = shrink(grad_up, "dp", dp, 0)
    for bit in range(2, low_bits - 1):
        grad_up = shrink(grad_up, "dp", dp, bit)
    summed_down = shrink(grad_down, "dp", dp, high)
    one_part = [
        terms[:own_rows] + swap(terms[own_rows:].astype(LOW), 0).astype(WIDE) for terms in one_terms
    ]
    grad_qkv = kept_qkv + sent_qkv.astype(WIDE)
    for bit in range(1, low_bits - 1):
        grad_qkv = shrink(grad_qkv, "dp", dp, bit)
    summed_out = shrink(grad_out, "dp", dp, high)
    grad_mod = jnp.concatenate([sum(one_sums), rest], axis=0)
    grad_mod = sum_all(grad_mod, "tensor", tp).astype(LOW)
    half = grad_qkv.shape[0] // 2
    kept_qkv, sent_qkv, one_part, grad_mod, summed_out, grad_up, summed_down = pin(
        grad_qkv[:half],
        grad_qkv[half:].astype(LOW),
        one_part,
        grad_mod,
        summed_out,
        grad_up,
        summed_down,
    )
    sent_qkv = flip(sent_qkv, "dp", dp, high)
    for bit in high_bits:
        one_part = [
            one_part[2 * k] + swap(one_part[2 * k + 1].astype(LOW), bit).astype(WIDE)
            for k in range(len(one_part) // 2)
        ]
    grad_mod = fold_features(grad_mod, "dp", dp, [0])
    grad_mod, grad_up = pin(grad_mod, grad_up)
    summed_up = shrink(grad_up, "dp", dp, high)
    part_total = jnp.sum(summed_down * summed_down) + jnp.sum(summed_out * summed_out)
    sent_qkv, grad_mod, one_part, part_total = pin(sent_qkv, grad_mod, one_part, part_total)
    grad_qkv = kept_qkv + sent_qkv.astype(WIDE)
    grad_mod = fold_features(grad_mod, "dp", dp, range(1, low_bits))
    summed_ada = jnp.einsum("pkn,pi->kni", grad_mod, signal_all, preferred_element_type=WIDE)
    summed_qkv = jnp.stack(
        [grad_qkv[:, t * heads_width : (t + 1) * heads_width] for t in range(3)], axis=0
    )
    part_total = part_total + jnp.sum(summed_up * summed_up)
    total = part_total + jnp.sum(grad_qkv * grad_qkv) + jnp.sum(summed_ada * summed_ada)

    input_grad = grad_middle[0] + normalize_back(
        norm_one[0][:own_rows], inverse_one[0][:own_rows], one_part[0] * (1.0 + scale_one)
    )
    coarse = input_grad.astype(LOW)
    fine = (input_grad - coarse.astype(WIDE)).astype(LOW)
    input_grad = matmul(coarse, select, ((1,), (1,))) + matmul(fine, select, ((1,), (1,)))
    grad_signal = jnp.einsum("pkn,kni->pi", grad_mod, low_ada, preferred_element_type=WIDE)
    total = sum_all(total, "tensor", tp)
    total, input_grad = pin(total, input_grad)
    total = sum_all(total, "dp", dp)
    total, grad_signal = pin(total, grad_signal)
    for bit in range(low_bits):
        rows = grad_signal.shape[0] // 2
        grad_signal = grad_signal[:rows] + flip(grad_signal[rows:], "dp", dp, bit)
    cond_grad = silu_back(grad_signal)[0]
    grad_norm = jnp.sqrt(total)
    clip_factor = CLIP_NORM / jnp.maximum(grad_norm, CLIP_NORM)
    qkv = adam_update(qkv_weight, summed_qkv, qkv_moment, qkv_square, clip_factor)
    out = adam_update(out_weight, summed_out, out_moment, out_square, clip_factor)
    up = adam_update(up_weight, summed_up, up_moment, up_square, clip_factor)
    down = adam_update(down_weight, summed_down, down_moment, down_square, clip_factor)
    ada = adam_update(ada_weight, summed_ada, ada_moment, ada_square, clip_factor)
    return (
        block_out[None],
        input_grad[None],
        cond_grad,
        grad_norm,
        *(new for group in zip(qkv, out, up, down, ada) for new in group),
    )


def solution(mesh):
    dp, tp = mesh.shape["dp"], mesh.shape["tensor"]
    rows = P("dp", "tensor", None)
    plain = P("dp", "tensor")
    stacked = P(None, "dp", "tensor")
    weights = (stacked, plain, plain, plain, stacked)

    def step(*arrays):
        return on_device(dp, tp, *arrays)

    return jax.shard_map(
        step,
        mesh=mesh,
        in_specs=(rows, plain, rows) + weights * 3,
        out_specs=(rows, rows, plain, P()) + weights * 3,
        check_vma=False,
    )
```

```python
import functools

import jax
import jax.numpy as jnp
import numpy as np
from jax import lax
from jax.experimental import pallas as pl
from jax.experimental.pallas import tpu as pltpu
from jax.sharding import PartitionSpec as P

HEAD_DIM = 72
SCORE_SCALE = HEAD_DIM ** (-0.5)
QUERY_ROWS = 256
COLUMN_BLOCK = 384
STEP = 10

EPS_NORM = 1e-06
CLIP_NORM = 1.0
LEARN_RATE = 0.05
WEIGHT_DECAY = 0.1
BETA_ONE = 0.9
BETA_TWO = 0.999
EPS_ADAM = 1e-08

LOW = jnp.bfloat16
WIDE = jnp.float32


def bit_count(size):
    return size.bit_length() - 1


def flip(value, axis, size, bit):
    return lax.ppermute(value, axis, [(i, i ^ (1 << bit)) for i in range(size)])


def grow(value, axis, size, bit):
    return jnp.concatenate([value, flip(value, axis, size, bit)], axis=0)


def shrink(value, axis, size, bit):
    half = value.shape[0] // 2
    moved = flip(value[half:].astype(LOW), axis, size, bit)
    return value[:half] + moved.astype(WIDE)


def gather_rel(value, axis, size):
    for bit in reversed(range(bit_count(size))):
        value = grow(value, axis, size, bit)
    return value


def scatter_rel(value, axis, size):
    for bit in range(bit_count(size)):
        value = shrink(value, axis, size, bit)
    return value


def spread_features(value, axis, size, bit):
    pairs = value.reshape((value.shape[0] // 2, 2) + value.shape[1:])
    moved = flip(pairs[:, 1], axis, size, bit)
    return jnp.concatenate([pairs[:, 0], moved], axis=-1)


def fold_features(value, axis, size, bits):
    if value.ndim == 2:
        value = value[None]
    for bit in bits:
        half = value.shape[-1] // 2
        moved = flip(value[..., half:], axis, size, bit)
        value = jnp.stack([value[..., :half], moved], axis=1)
        value = value.reshape((-1,) + value.shape[2:])
    return value


def sum_all(value, axis, size):
    for bit in range(bit_count(size)):
        value = value + flip(value, axis, size, bit)
    return value


def pin(*values):
    return lax.optimization_barrier(values)


def reversed_bits(size):
    bits = bit_count(size)
    return np.array([int(format(i, f"0{bits}b")[::-1], 2) if bits else 0 for i in range(size)])


def selection(index, size, width):
    block = width // size
    place = np.arange(width)
    source = (index ^ jnp.asarray(reversed_bits(size)[place // block], jnp.int32)) * block
    source = source + jnp.asarray(place % block, jnp.int32)
    return (lax.broadcasted_iota(jnp.int32, (width, width), 0) == source[None, :]).astype(LOW)


def matmul(left, right, dims):
    return lax.dot_general(left, right, (dims, ((), ())), preferred_element_type=WIDE)


def normalize(values):
    centre = values - jnp.mean(values, axis=-1, keepdims=True)
    spread = jnp.mean(centre * centre, axis=-1, keepdims=True)
    inverse = lax.rsqrt(spread + EPS_NORM)
    return centre * inverse, inverse


def normalize_back(normed, inverse, grad):
    mean_grad = jnp.mean(grad, axis=-1, keepdims=True)
    mean_both = jnp.mean(grad * normed, axis=-1, keepdims=True)
    return inverse * (grad - mean_grad - normed * mean_both)


def gelu_tanh(values):
    return jax.nn.gelu(values, approximate=True)


def work(flops, weight):
    return pl.CostEstimate(flops=weight * flops, bytes_accessed=1 << 20, transcendentals=0)


def attend_kernel(query_ref, all_ref, out_ref, log_ref):
    heads_width = out_ref.shape[1]
    for head in range(heads_width // HEAD_DIM):
        place = head * HEAD_DIM
        queries = query_ref[:, place : place + HEAD_DIM]
        keys = all_ref[:, heads_width + place : heads_width + place + HEAD_DIM]
        values = all_ref[:, 2 * heads_width + place : 2 * heads_width + place + HEAD_DIM]
        scores = matmul(keys, queries, ((1,), (1,)))
        peak = jnp.max(scores, axis=0, keepdims=True)
        exponent = jnp.exp((scores - peak) * SCORE_SCALE)
        total = jnp.sum(exponent, axis=0, keepdims=True)
        probability = (exponent * (1.0 / total)).astype(LOW)
        mixture = matmul(values, probability, ((0,), (0,)))
        out_ref[:, place : place + HEAD_DIM] = mixture.T.astype(LOW)
        log_ref[head : head + 1, :] = peak * SCORE_SCALE + jnp.log(total)


def attend(projected, chunk, chunk_rows):
    length, all_width = projected.shape
    heads_width = all_width // 3
    rows = min(QUERY_ROWS, chunk_rows)
    start = chunk * chunk_rows // rows
    return pl.pallas_call(
        attend_kernel,
        grid=(chunk_rows // rows,),
        in_specs=[
            pl.BlockSpec((rows, all_width), lambda i: (start + i, 0)),
            pl.BlockSpec((length, all_width), lambda i: (0, 0)),
        ],
        out_specs=[
            pl.BlockSpec((rows, heads_width), lambda i: (i, 0)),
            pl.BlockSpec((heads_width // HEAD_DIM, rows), lambda i: (0, i)),
        ],
        out_shape=[
            jax.ShapeDtypeStruct((chunk_rows, heads_width), LOW),
            jax.ShapeDtypeStruct((heads_width // HEAD_DIM, chunk_rows), WIDE),
        ],
        compiler_params=pltpu.CompilerParams(vmem_limit_bytes=24 << 20),
        cost_estimate=work(4 * chunk_rows * length * heads_width, 4),
        name="attend",
    )(projected, projected)


def attend_back_kernel(query_ref, all_ref, log_ref, grad_ref, out_ref, key_sum, value_sum):
    heads_width = grad_ref.shape[1]
    rows = query_ref.shape[0]
    step = pl.program_id(0)

    @pl.when(step == 0)
    def _():
        key_sum[...] = jnp.zeros_like(key_sum)
        value_sum[...] = jnp.zeros_like(value_sum)

    for head in range(heads_width // HEAD_DIM):
        place = head * HEAD_DIM
        queries = query_ref[:, place : place + HEAD_DIM]
        keys = all_ref[:, heads_width + place : heads_width + place + HEAD_DIM]
        values = all_ref[:, 2 * heads_width + place : 2 * heads_width + place + HEAD_DIM]
        grads = grad_ref[:, place : place + HEAD_DIM]
        scores = matmul(keys, queries, ((1,), (1,)))
        probability = jnp.exp(scores * SCORE_SCALE - log_ref[head : head + 1, :])
        grad_probability = matmul(values, grads, ((1,), (1,)))
        inner = jnp.sum(probability * grad_probability, axis=0, keepdims=True)
        grad_scores = (probability * (grad_probability - inner)).astype(LOW)
        key_sum[head] += matmul(grad_scores, queries, ((1,), (0,)))
        value_sum[head] += matmul(probability.astype(LOW), grads, ((1,), (0,)))
        grad_query = matmul(keys, grad_scores, ((0,), (0,))) * SCORE_SCALE
        out_ref[pl.ds(pl.multiple_of(step * rows, rows), rows), place : place + HEAD_DIM] = (
            grad_query.T.astype(LOW)
        )

    @pl.when(step == pl.num_programs(0) - 1)
    def _():
        for head in range(heads_width // HEAD_DIM):
            place = heads_width + head * HEAD_DIM
            out_ref[:, place : place + HEAD_DIM] = (key_sum[head] * SCORE_SCALE).astype(LOW)
            place += heads_width
            out_ref[:, place : place + HEAD_DIM] = value_sum[head].astype(LOW)


def attend_back(projected, log_totals, grad_attended):
    length, all_width = projected.shape
    heads_width = all_width // 3
    heads = heads_width // HEAD_DIM
    rows = min(QUERY_ROWS, length)
    return pl.pallas_call(
        attend_back_kernel,
        grid=(length // rows,),
        in_specs=[
            pl.BlockSpec((rows, all_width), lambda i: (i, 0)),
            pl.BlockSpec((length, all_width), lambda i: (0, 0)),
            pl.BlockSpec((heads, rows), lambda i: (0, i)),
            pl.BlockSpec((rows, heads_width), lambda i: (i, 0)),
        ],
        out_specs=pl.BlockSpec((length, all_width), lambda i: (0, 0)),
        out_shape=jax.ShapeDtypeStruct((length, all_width), LOW),
        scratch_shapes=[
            pltpu.VMEM((heads, length, HEAD_DIM), WIDE),
            pltpu.VMEM((heads, length, HEAD_DIM), WIDE),
        ],
        compiler_params=pltpu.CompilerParams(vmem_limit_bytes=36 << 20),
        cost_estimate=work(10 * length * length * heads_width, 2),
        name="attend_back",
    )(projected, projected, log_totals, grad_attended)


def token_terms_kernel(grad_ref, weight_ref, norm_ref, terms_ref, sums_ref):
    terms = matmul(grad_ref[...], weight_ref[...], ((1,), (1,)))
    terms_ref[...] = terms

    @pl.when(pl.program_id(0) == 0)
    def _():
        sums_ref[...] = jnp.zeros_like(sums_ref)

    sums_ref[0:1] += jnp.sum(terms, axis=0, keepdims=True)
    sums_ref[1:2] += jnp.sum(terms * norm_ref[...], axis=0, keepdims=True)


def token_terms(grads, weight, normed, chunk):
    chunk_rows, width = normed.shape
    rows = min(QUERY_ROWS, chunk_rows)
    start = chunk * chunk_rows // rows
    return pl.pallas_call(
        token_terms_kernel,
        grid=(chunk_rows // rows,),
        in_specs=[
            pl.BlockSpec((rows, grads.shape[1]), lambda i: (start + i, 0)),
            pl.BlockSpec(weight.shape, lambda i: (0, 0)),
            pl.BlockSpec((rows, width), lambda i: (i, 0)),
        ],
        out_specs=[
            pl.BlockSpec((rows, width), lambda i: (i, 0)),
            pl.BlockSpec((2, width), lambda i: (0, 0)),
        ],
        out_shape=[
            jax.ShapeDtypeStruct((chunk_rows, width), WIDE),
            jax.ShapeDtypeStruct((2, width), WIDE),
        ],
        compiler_params=pltpu.CompilerParams(vmem_limit_bytes=24 << 20),
        cost_estimate=work(2 * chunk_rows * width * grads.shape[1], 1),
        name="token_terms",
    )(grads, weight, normed)


def weight_grad_kernel(pairs, *refs):
    parts = (len(refs) - 2) // 2
    lefts, rights, (kept_ref, sent_ref) = refs[:parts], refs[parts:-2], refs[-2:]
    split, columns = kept_ref.shape
    turned = [left[...].T for left in lefts]
    for start in range(0, columns, COLUMN_BLOCK):
        stop = min(start + COLUMN_BLOCK, columns)
        total = sum(
            matmul(left, right[:, start:stop], ((1,), (0,))) for left, right in zip(turned, rights)
        )
        rows = split // pairs
        for k in range(pairs):
            place = slice(k * rows, (k + 1) * rows)
            kept_ref[place, start:stop] = total[2 * k * rows : (2 * k + 1) * rows]
            sent_ref[place, start:stop] = total[(2 * k + 1) * rows : (2 * k + 2) * rows].astype(LOW)


def weight_grad(lefts, rights, pairs=1):
    split, columns = lefts[0].shape[1] // 2, rights[0].shape[1]
    return pl.pallas_call(
        functools.partial(weight_grad_kernel, pairs),
        out_shape=[
            jax.ShapeDtypeStruct((split, columns), WIDE),
            jax.ShapeDtypeStruct((split, columns), LOW),
        ],
        compiler_params=pltpu.CompilerParams(vmem_limit_bytes=40 << 20),
        cost_estimate=work(4 * sum(left.shape[0] for left in lefts) * split * columns, 1),
        name="weight_grad",
    )(*lefts, *rights)


def adam_update(weight, gradient, moment, square, clip_factor):
    clipped = gradient * clip_factor
    moment_new = BETA_ONE * moment + (1.0 - BETA_ONE) * clipped
    square_new = BETA_TWO * square + (1.0 - BETA_TWO) * clipped * clipped
    mean_hat = moment_new / (1.0 - BETA_ONE**STEP)
    square_hat = square_new / (1.0 - BETA_TWO**STEP)
    weight_new = weight - LEARN_RATE * (
        mean_hat / (jnp.sqrt(square_hat) + EPS_ADAM) + WEIGHT_DECAY * weight
    )
    return (weight_new, moment_new, square_new)


def on_device(
    dp,
    tp,
    tokens,
    conditioning,
    out_grad,
    qkv_weight,
    out_weight,
    up_weight,
    down_weight,
    ada_weight,
    qkv_moment,
    out_moment,
    up_moment,
    down_moment,
    ada_moment,
    qkv_square,
    out_square,
    up_square,
    down_square,
    ada_square,
):
    width = tokens.shape[-1]
    heads_width = out_weight.shape[-1]
    here = lax.axis_index("dp")
    select = selection(here, dp, width)
    low_bits = bit_count(dp)
    high_bits = range(1, bit_count(tp))
    chunks = range(tp // 2)

    def swap(value, bit):
        return flip(value, "tensor", tp, bit)

    def widen(value):
        return jnp.concatenate([value, swap(value, 0)], axis=0)

    def all_blocks(value):
        pieces = [value]
        for bit in reversed(high_bits):
            pieces = pieces + [swap(piece, bit) for piece in pieces]
        return pieces

    def token_sum(kept, sent):
        return high_sum([keep + swap(send, 0).astype(WIDE) for keep, send in zip(kept, sent)])

    def high_sum(part):
        for bit in high_bits:
            low_part = [value.astype(LOW) for value in part]
            moved = [swap(value, bit) for value in low_part]
            part = [
                low_part[k].astype(WIDE) + moved[k ^ (1 << (bit - 1))].astype(WIDE) for k in chunks
            ]
        return part

    def split_product(left, right, dims):
        rows = left.shape[0] // 2
        return pin(matmul(left[:rows], right, dims), matmul(left[rows:], right, dims).astype(LOW))

    signal, silu_back = jax.vjp(jax.nn.silu, conditioning)
    low_ada = ada_weight.astype(LOW)
    high, middle_bits = low_bits - 1, list(reversed(range(1, low_bits - 1)))

    def grow_all(value, bits):
        for bit in bits:
            value = grow(value, "dp", dp, bit)
        return value

    signal_all = grow(signal.astype(LOW), "dp", dp, high)
    full_qkv = jnp.concatenate([qkv_weight[t].astype(LOW) for t in range(3)], axis=1)
    signal_all, full_qkv = pin(signal_all, full_qkv)
    full_qkv = grow(full_qkv, "dp", dp, high)
    own_tokens = matmul(tokens[0], select, ((1,), (0,))).astype(LOW)
    own_grad = matmul(out_grad[0], select, ((1,), (0,))).astype(LOW)
    signal_all = grow_all(signal_all, middle_bits + [0])
    tokens_low = all_blocks(own_tokens)
    modulation = jnp.einsum("pi,kni->pkn", signal_all, low_ada, preferred_element_type=WIDE)
    modulation, full_qkv = pin(modulation, full_qkv)
    full_qkv = grow_all(full_qkv, middle_bits)
    modulation = sum_all(modulation, "tensor", tp)
    count = modulation.shape[0] // 2
    moved = flip(modulation[count:], "dp", dp, 0)
    modulation = jnp.concatenate([modulation[:count], moved], axis=-1)
    modulation, full_qkv, tokens_low, own_grad = pin(modulation, full_qkv, tokens_low, own_grad)
    full_qkv = grow(full_qkv, "dp", dp, 0)
    tokens_low = [widen(piece) for piece in tokens_low]
    for bit in [high] + middle_bits:
        modulation = spread_features(modulation, "dp", dp, bit)
    piece = width // dp
    modulation = jnp.concatenate(
        [
            modulation[0, :, (2 * k + low_bit) * piece : (2 * k + low_bit + 1) * piece]
            for low_bit in range(2)
            for k in range(dp // 2)
        ],
        axis=-1,
    )
    modulation = modulation.reshape(6, 1, width)
    shift_one, scale_one, gate_one, shift_two, scale_two, gate_two = modulation

    tokens_wide = [value.astype(WIDE) for value in tokens_low]
    norm_one, inverse_one = zip(*(pin(*normalize(value)) for value in tokens_wide))
    normed_one = [(value * (1.0 + scale_one) + shift_one).astype(LOW) for value in norm_one]
    normed_one = jnp.concatenate(normed_one, axis=0)
    lows = [weight.astype(LOW) for weight in (out_weight, up_weight, down_weight)]
    normed_one, own_grad, (full_out, full_up, full_down) = pin(normed_one, own_grad, lows)
    grad_low = all_blocks(own_grad)
    full_out = grow(full_out, "dp", dp, high)
    full_out, full_up = pin(full_out, full_up)
    full_out = grow_all(full_out, middle_bits)
    full_up = grow(full_up, "dp", dp, high)
    full_qkv, full_out, full_down = pin(full_qkv, full_out, full_down)
    full_out = grow(full_out, "dp", dp, 0)
    full_down = grow(full_down, "dp", dp, high)
    projected = matmul(normed_one, full_qkv, ((1,), (0,))).astype(LOW)
    length = projected.shape[0]
    chunk_rows = length // len(chunks)
    attended, log_totals, part = [], [], []
    for k in chunks:
        mixed, log_total = attend(projected, k, chunk_rows)
        if k == 0:
            mixed, full_out, full_up, full_down = pin(mixed, full_out, full_up, full_down)
            full_down = grow_all(full_down, middle_bits)
            full_up = grow_all(full_up, middle_bits[:-1] + [0])
        keep, send = split_product(mixed, full_out, ((1,), (1,)))
        part.append(keep + swap(send, 0).astype(WIDE))
        part[k], projected = pin(part[k], projected)
        attended.append(mixed)
        log_totals.append(log_total)
    part, full_up, full_down = pin(part, full_up, full_down)
    moved_up = flip(full_up, "dp", dp, middle_bits[-1])
    moved_down = flip(full_down, "dp", dp, 0)
    attn_rows = high_sum(part)
    attn_rows, moved_up, moved_down, grad_low = pin(attn_rows, moved_up, moved_down, grad_low)
    grad_low = [widen(piece) for piece in grad_low]
    own_rows = attn_rows[0].shape[0]
    middle = [tokens_wide[k][:own_rows] + gate_one * attn_rows[k] for k in chunks]
    norm_two, inverse_two = zip(*(normalize(value) for value in middle))
    normed_two = [(value * (1.0 + scale_two) + shift_two).astype(LOW) for value in norm_two]
    seq_two = [widen(value) for value in normed_two]
    rows = full_up.shape[0] // 2
    full_up = jnp.concatenate(
        [full_up[:rows], moved_up[:rows], full_up[rows:], moved_up[rows:]], axis=0
    )
    full_down = jnp.concatenate([full_down, moved_down], axis=0)

    pre_act = [matmul(part, full_up, ((1,), (0,))) for part in seq_two]
    activated, gelu_back = zip(*(jax.vjp(gelu_tanh, part) for part in pre_act))
    hidden = [part.astype(LOW) for part in activated]

    grad_mlp = [(part.astype(WIDE) * gate_two).astype(LOW) for part in grad_low]
    kept_down, sent_down = weight_grad(grad_mlp, hidden)
    kept_down, sent_down, grad_mlp, hidden = pin(kept_down, sent_down, grad_mlp, hidden)
    sent_down = flip(sent_down, "dp", dp, 0)
    grad_hidden = [matmul(part, full_down, ((1,), (0,))) for part in grad_mlp]
    grad_pre = [back(part)[0].astype(LOW) for back, part in zip(gelu_back, grad_hidden)]
    part = []
    for k in chunks:
        keep, send = split_product(grad_pre[k], full_up, ((1,), (1,)))
        part.append(keep + swap(send, 0).astype(WIDE))
    part, grad_pre, seq_two = pin(part, grad_pre, seq_two)
    kept_up, sent_up = weight_grad(seq_two, grad_pre, 2)
    grad_normed_two = high_sum(part)
    grad_normed_two[0], kept_up, sent_up, sent_down = pin(
        grad_normed_two[0], kept_up, sent_up, sent_down
    )
    grad_down = kept_down + sent_down.astype(WIDE)
    for bit in range(1, low_bits - 1):
        grad_down = shrink(grad_down, "dp", dp, bit)

    grad_shift_two = jnp.sum(grad_normed_two[0], axis=0)
    grad_scale_two = jnp.sum(grad_normed_two[0] * norm_two[0], axis=0)
    grad_middle = [
        grad_low[k][:own_rows].astype(WIDE)
        + normalize_back(norm_two[k], inverse_two[k], grad_normed_two[k] * (1.0 + scale_two))
        for k in chunks
    ]
    grad_gate_one = jnp.sum(grad_middle[0] * attn_rows[0], axis=0)

    grad_attn = [widen((part * gate_one).astype(LOW)) for part in grad_middle]
    grad_attended = [
        matmul(part, full_out, ((1,), (0,))).astype(LOW)
        for part in grad_attn
    ]
    kept_out, sent_out = weight_grad(grad_attn, attended)
    kept_out, sent_out, grad_attended = pin(kept_out, sent_out, grad_attended)
    sent_up = flip(sent_up, "dp", dp, 1)
    sent_out = flip(sent_out, "dp", dp, 0)
    grad_projected = attend_back(
        projected, jnp.concatenate(log_totals, axis=1), jnp.concatenate(grad_attended, axis=0)
    )

    grad_projected, sent_out, grad_down = pin(grad_projected, sent_out, grad_down)
    summed_down = shrink(grad_down, "dp", dp, high)
    grad_out = kept_out + sent_out.astype(WIDE)
    kept_qkv, sent_qkv = weight_grad([normed_one], [grad_projected])
    kept_qkv, sent_qkv, grad_projected, hidden = pin(kept_qkv, sent_qkv, grad_projected, hidden)
    sent_qkv = flip(sent_qkv, "dp", dp, 0)
    mlp_kept, mlp_sent = zip(*(split_product(part, full_down, ((1,), (1,))) for part in hidden))
    mlp_part = [keep + swap(send, 0).astype(WIDE) for keep, send in zip(mlp_kept, mlp_sent)]
    mlp_part, grad_projected = pin(mlp_part, grad_projected)
    for bit in high_bits:
        mlp_part = [
            mlp_part[2 * k] + swap(mlp_part[2 * k + 1].astype(LOW), bit).astype(WIDE)
            for k in range(len(mlp_part) // 2)
        ]
    mlp_rows = mlp_part[0]
    block_out = (middle[0] + gate_two * mlp_rows).astype(LOW)
    block_out = matmul(block_out, select, ((1,), (1,))).astype(LOW)
    grad_gate_two = jnp.sum(own_grad.astype(WIDE) * mlp_rows, axis=0)
    one_terms, one_sums = zip(
        *(token_terms(grad_projected, full_qkv, norm_one[k], k) for k in chunks)
    )
    rest = jnp.stack([grad_gate_one, grad_shift_two, grad_scale_two, grad_gate_two])
    one_sums, one_terms, sent_qkv, rest, sent_up, grad_out = pin(
        one_sums, one_terms, sent_qkv, rest, sent_up, grad_out
    )
    for bit in range(1, low_bits - 1):
        grad_out = shrink(grad_out, "dp", dp, bit)
    grad_up = kept_up + sent_up.astype(WIDE)
    grad_up = shrink(grad_up, "dp", dp, 0)
    for bit in range(2, low_bits - 1):
        grad_up = shrink(grad_up, "dp", dp, bit)
    one_part = [
        terms[:own_rows] + swap(terms[own_rows:].astype(LOW), 0).astype(WIDE) for terms in one_terms
    ]
    grad_qkv = kept_qkv + sent_qkv.astype(WIDE)
    for bit in range(1, low_bits - 1):
        grad_qkv = shrink(grad_qkv, "dp", dp, bit)
    grad_mod = jnp.concatenate([sum(one_sums), rest], axis=0)
    grad_mod = sum_all(grad_mod, "tensor", tp).astype(LOW)
    half = grad_qkv.shape[0] // 2
    kept_qkv, sent_qkv, one_part, grad_mod, block_out, grad_out, summed_down = pin(
        grad_qkv[:half],
        grad_qkv[half:].astype(LOW),
        one_part,
        grad_mod,
        block_out,
        grad_out,
        summed_down,
    )
    summed_out = shrink(grad_out, "dp", dp, high)
    sent_qkv = flip(sent_qkv, "dp", dp, high)
    for bit in high_bits:
        one_part = [
            one_part[2 * k] + swap(one_part[2 * k + 1].astype(LOW), bit).astype(WIDE)
            for k in range(len(one_part) // 2)
        ]
    grad_mod = fold_features(grad_mod, "dp", dp, [0])
    part_total = jnp.sum(summed_down * summed_down)
    sent_qkv, grad_mod, one_part, part_total, grad_up, summed_out = pin(
        sent_qkv, grad_mod, one_part, part_total, grad_up, summed_out
    )
    summed_up = shrink(grad_up, "dp", dp, high)
    part_total = part_total + jnp.sum(summed_out * summed_out)
    grad_qkv = kept_qkv + sent_qkv.astype(WIDE)
    grad_mod = fold_features(grad_mod, "dp", dp, range(1, low_bits))
    summed_ada = jnp.einsum("pkn,pi->kni", grad_mod, signal_all, preferred_element_type=WIDE)
    summed_qkv = jnp.stack(
        [grad_qkv[:, t * heads_width : (t + 1) * heads_width] for t in range(3)], axis=0
    )
    part_total = part_total + jnp.sum(summed_up * summed_up)
    total = part_total + jnp.sum(grad_qkv * grad_qkv) + jnp.sum(summed_ada * summed_ada)

    input_grad = grad_middle[0] + normalize_back(
        norm_one[0][:own_rows], inverse_one[0][:own_rows], one_part[0] * (1.0 + scale_one)
    )
    coarse = input_grad.astype(LOW)
    fine = (input_grad - coarse.astype(WIDE)).astype(LOW)
    input_grad = matmul(coarse, select, ((1,), (1,))) + matmul(fine, select, ((1,), (1,)))
    grad_signal = jnp.einsum("pkn,kni->pi", grad_mod, low_ada, preferred_element_type=WIDE)
    total = sum_all(total, "tensor", tp)
    total, input_grad = pin(total, input_grad)
    for bit in range(low_bits):
        rows = grad_signal.shape[0] // 2
        row = jnp.broadcast_to(total, (1, grad_signal.shape[1]))
        sent = jnp.concatenate([grad_signal[rows:], row], axis=0)
        moved = flip(sent, "dp", dp, bit)
        grad_signal = grad_signal[:rows] + moved[:rows]
        total = total + moved[rows, 0]
    cond_grad = silu_back(grad_signal)[0]
    grad_norm = jnp.sqrt(total)
    clip_factor = CLIP_NORM / jnp.maximum(grad_norm, CLIP_NORM)
    qkv = adam_update(qkv_weight, summed_qkv, qkv_moment, qkv_square, clip_factor)
    out = adam_update(out_weight, summed_out, out_moment, out_square, clip_factor)
    up = adam_update(up_weight, summed_up, up_moment, up_square, clip_factor)
    down = adam_update(down_weight, summed_down, down_moment, down_square, clip_factor)
    ada = adam_update(ada_weight, summed_ada, ada_moment, ada_square, clip_factor)
    return (
        block_out[None],
        input_grad[None],
        cond_grad,
        grad_norm,
        *(new for group in zip(qkv, out, up, down, ada) for new in group),
    )


def solution(mesh):
    dp, tp = mesh.shape["dp"], mesh.shape["tensor"]
    rows = P("dp", "tensor", None)
    plain = P("dp", "tensor")
    stacked = P(None, "dp", "tensor")
    weights = (stacked, plain, plain, plain, stacked)

    def step(*arrays):
        return on_device(dp, tp, *arrays)

    return jax.shard_map(
        step,
        mesh=mesh,
        in_specs=(rows, plain, rows) + weights * 3,
        out_specs=(rows, rows, plain, P()) + weights * 3,
        check_vma=False,
    )
```

```python
import functools

import jax
import jax.numpy as jnp
import numpy as np
from jax import lax
from jax.experimental import pallas as pl
from jax.experimental.pallas import tpu as pltpu
from jax.sharding import PartitionSpec as P

HEAD_DIM = 72
SCORE_SCALE = HEAD_DIM ** (-0.5)
QUERY_ROWS = 256
COLUMN_BLOCK = 384
STEP = 10

EPS_NORM = 1e-06
CLIP_NORM = 1.0
LEARN_RATE = 0.05
WEIGHT_DECAY = 0.1
BETA_ONE = 0.9
BETA_TWO = 0.999
EPS_ADAM = 1e-08

LOW = jnp.bfloat16
WIDE = jnp.float32


def bit_count(size):
    return size.bit_length() - 1


def flip(value, axis, size, bit):
    return lax.ppermute(value, axis, [(i, i ^ (1 << bit)) for i in range(size)])


def grow(value, axis, size, bit):
    return jnp.concatenate([value, flip(value, axis, size, bit)], axis=0)


def shrink(value, axis, size, bit):
    half = value.shape[0] // 2
    moved = flip(value[half:].astype(LOW), axis, size, bit)
    return value[:half] + moved.astype(WIDE)


def gather_rel(value, axis, size):
    for bit in reversed(range(bit_count(size))):
        value = grow(value, axis, size, bit)
    return value


def scatter_rel(value, axis, size):
    for bit in range(bit_count(size)):
        value = shrink(value, axis, size, bit)
    return value


def spread_features(value, axis, size, bit):
    pairs = value.reshape((value.shape[0] // 2, 2) + value.shape[1:])
    moved = flip(pairs[:, 1], axis, size, bit)
    return jnp.concatenate([pairs[:, 0], moved], axis=-1)


def fold_features(value, axis, size, bits):
    if value.ndim == 2:
        value = value[None]
    for bit in bits:
        half = value.shape[-1] // 2
        moved = flip(value[..., half:], axis, size, bit)
        value = jnp.stack([value[..., :half], moved], axis=1)
        value = value.reshape((-1,) + value.shape[2:])
    return value


def sum_all(value, axis, size):
    for bit in range(bit_count(size)):
        value = value + flip(value, axis, size, bit)
    return value


def pin(*values):
    return lax.optimization_barrier(values)


def reversed_bits(size):
    bits = bit_count(size)
    return np.array([int(format(i, f"0{bits}b")[::-1], 2) if bits else 0 for i in range(size)])


def selection(index, size, width):
    block = width // size
    place = np.arange(width)
    source = (index ^ jnp.asarray(reversed_bits(size)[place // block], jnp.int32)) * block
    source = source + jnp.asarray(place % block, jnp.int32)
    return (lax.broadcasted_iota(jnp.int32, (width, width), 0) == source[None, :]).astype(LOW)


def matmul(left, right, dims):
    return lax.dot_general(left, right, (dims, ((), ())), preferred_element_type=WIDE)


def normalize(values):
    centre = values - jnp.mean(values, axis=-1, keepdims=True)
    spread = jnp.mean(centre * centre, axis=-1, keepdims=True)
    inverse = lax.rsqrt(spread + EPS_NORM)
    return centre * inverse, inverse


def normalize_back(normed, inverse, grad):
    mean_grad = jnp.mean(grad, axis=-1, keepdims=True)
    mean_both = jnp.mean(grad * normed, axis=-1, keepdims=True)
    return inverse * (grad - mean_grad - normed * mean_both)


def gelu_tanh(values):
    return jax.nn.gelu(values, approximate=True)


def work(flops, weight):
    return pl.CostEstimate(flops=weight * flops, bytes_accessed=1 << 20, transcendentals=0)


def attend_kernel(query_ref, all_ref, out_ref, log_ref):
    heads_width = out_ref.shape[1]
    for head in range(heads_width // HEAD_DIM):
        place = head * HEAD_DIM
        queries = query_ref[:, place : place + HEAD_DIM]
        keys = all_ref[:, heads_width + place : heads_width + place + HEAD_DIM]
        values = all_ref[:, 2 * heads_width + place : 2 * heads_width + place + HEAD_DIM]
        scores = matmul(keys, queries, ((1,), (1,)))
        peak = jnp.max(scores, axis=0, keepdims=True)
        exponent = jnp.exp((scores - peak) * SCORE_SCALE)
        total = jnp.sum(exponent, axis=0, keepdims=True)
        probability = (exponent * (1.0 / total)).astype(LOW)
        mixture = matmul(values, probability, ((0,), (0,)))
        out_ref[:, place : place + HEAD_DIM] = mixture.T.astype(LOW)
        log_ref[head : head + 1, :] = peak * SCORE_SCALE + jnp.log(total)


def attend(projected, chunk, chunk_rows):
    length, all_width = projected.shape
    heads_width = all_width // 3
    rows = min(QUERY_ROWS, chunk_rows)
    start = chunk * chunk_rows // rows
    return pl.pallas_call(
        attend_kernel,
        grid=(chunk_rows // rows,),
        in_specs=[
            pl.BlockSpec((rows, all_width), lambda i: (start + i, 0)),
            pl.BlockSpec((length, all_width), lambda i: (0, 0)),
        ],
        out_specs=[
            pl.BlockSpec((rows, heads_width), lambda i: (i, 0)),
            pl.BlockSpec((heads_width // HEAD_DIM, rows), lambda i: (0, i)),
        ],
        out_shape=[
            jax.ShapeDtypeStruct((chunk_rows, heads_width), LOW),
            jax.ShapeDtypeStruct((heads_width // HEAD_DIM, chunk_rows), WIDE),
        ],
        compiler_params=pltpu.CompilerParams(vmem_limit_bytes=24 << 20),
        cost_estimate=work(4 * chunk_rows * length * heads_width, 4),
        name="attend",
    )(projected, projected)


def attend_back_kernel(query_ref, all_ref, log_ref, grad_ref, out_ref, key_sum, value_sum):
    heads_width = grad_ref.shape[1]
    rows = query_ref.shape[0]
    step = pl.program_id(0)

    @pl.when(step == 0)
    def _():
        key_sum[...] = jnp.zeros_like(key_sum)
        value_sum[...] = jnp.zeros_like(value_sum)

    for head in range(heads_width // HEAD_DIM):
        place = head * HEAD_DIM
        queries = query_ref[:, place : place + HEAD_DIM]
        keys = all_ref[:, heads_width + place : heads_width + place + HEAD_DIM]
        values = all_ref[:, 2 * heads_width + place : 2 * heads_width + place + HEAD_DIM]
        grads = grad_ref[:, place : place + HEAD_DIM]
        scores = matmul(keys, queries, ((1,), (1,)))
        probability = jnp.exp(scores * SCORE_SCALE - log_ref[head : head + 1, :])
        grad_probability = matmul(values, grads, ((1,), (1,)))
        inner = jnp.sum(probability * grad_probability, axis=0, keepdims=True)
        grad_scores = (probability * (grad_probability - inner)).astype(LOW)
        key_sum[head] += matmul(grad_scores, queries, ((1,), (0,)))
        value_sum[head] += matmul(probability.astype(LOW), grads, ((1,), (0,)))
        grad_query = matmul(keys, grad_scores, ((0,), (0,))) * SCORE_SCALE
        out_ref[pl.ds(pl.multiple_of(step * rows, rows), rows), place : place + HEAD_DIM] = (
            grad_query.T.astype(LOW)
        )

    @pl.when(step == pl.num_programs(0) - 1)
    def _():
        for head in range(heads_width // HEAD_DIM):
            place = heads_width + head * HEAD_DIM
            out_ref[:, place : place + HEAD_DIM] = (key_sum[head] * SCORE_SCALE).astype(LOW)
            place += heads_width
            out_ref[:, place : place + HEAD_DIM] = value_sum[head].astype(LOW)


def attend_back(projected, log_totals, grad_attended):
    length, all_width = projected.shape
    heads_width = all_width // 3
    heads = heads_width // HEAD_DIM
    rows = min(QUERY_ROWS, length)
    return pl.pallas_call(
        attend_back_kernel,
        grid=(length // rows,),
        in_specs=[
            pl.BlockSpec((rows, all_width), lambda i: (i, 0)),
            pl.BlockSpec((length, all_width), lambda i: (0, 0)),
            pl.BlockSpec((heads, rows), lambda i: (0, i)),
            pl.BlockSpec((rows, heads_width), lambda i: (i, 0)),
        ],
        out_specs=pl.BlockSpec((length, all_width), lambda i: (0, 0)),
        out_shape=jax.ShapeDtypeStruct((length, all_width), LOW),
        scratch_shapes=[
            pltpu.VMEM((heads, length, HEAD_DIM), WIDE),
            pltpu.VMEM((heads, length, HEAD_DIM), WIDE),
        ],
        compiler_params=pltpu.CompilerParams(vmem_limit_bytes=36 << 20),
        cost_estimate=work(10 * length * length * heads_width, 2),
        name="attend_back",
    )(projected, projected, log_totals, grad_attended)


def token_terms_kernel(grad_ref, weight_ref, norm_ref, terms_ref, sums_ref):
    terms = matmul(grad_ref[...], weight_ref[...], ((1,), (1,)))
    terms_ref[...] = terms

    @pl.when(pl.program_id(0) == 0)
    def _():
        sums_ref[...] = jnp.zeros_like(sums_ref)

    sums_ref[0:1] += jnp.sum(terms, axis=0, keepdims=True)
    sums_ref[1:2] += jnp.sum(terms * norm_ref[...], axis=0, keepdims=True)


def token_terms(grads, weight, normed, chunk):
    chunk_rows, width = normed.shape
    rows = min(QUERY_ROWS, chunk_rows)
    start = chunk * chunk_rows // rows
    return pl.pallas_call(
        token_terms_kernel,
        grid=(chunk_rows // rows,),
        in_specs=[
            pl.BlockSpec((rows, grads.shape[1]), lambda i: (start + i, 0)),
            pl.BlockSpec(weight.shape, lambda i: (0, 0)),
            pl.BlockSpec((rows, width), lambda i: (i, 0)),
        ],
        out_specs=[
            pl.BlockSpec((rows, width), lambda i: (i, 0)),
            pl.BlockSpec((2, width), lambda i: (0, 0)),
        ],
        out_shape=[
            jax.ShapeDtypeStruct((chunk_rows, width), WIDE),
            jax.ShapeDtypeStruct((2, width), WIDE),
        ],
        compiler_params=pltpu.CompilerParams(vmem_limit_bytes=24 << 20),
        cost_estimate=work(2 * chunk_rows * width * grads.shape[1], 1),
        name="token_terms",
    )(grads, weight, normed)


def weight_grad_kernel(pairs, *refs):
    parts = (len(refs) - 2) // 2
    lefts, rights, (kept_ref, sent_ref) = refs[:parts], refs[parts:-2], refs[-2:]
    split, columns = kept_ref.shape
    turned = [left[...].T for left in lefts]
    for start in range(0, columns, COLUMN_BLOCK):
        stop = min(start + COLUMN_BLOCK, columns)
        total = sum(
            matmul(left, right[:, start:stop], ((1,), (0,))) for left, right in zip(turned, rights)
        )
        rows = split // pairs
        for k in range(pairs):
            place = slice(k * rows, (k + 1) * rows)
            kept_ref[place, start:stop] = total[2 * k * rows : (2 * k + 1) * rows]
            sent_ref[place, start:stop] = total[(2 * k + 1) * rows : (2 * k + 2) * rows].astype(LOW)


def weight_grad(lefts, rights, pairs=1):
    split, columns = lefts[0].shape[1] // 2, rights[0].shape[1]
    return pl.pallas_call(
        functools.partial(weight_grad_kernel, pairs),
        out_shape=[
            jax.ShapeDtypeStruct((split, columns), WIDE),
            jax.ShapeDtypeStruct((split, columns), LOW),
        ],
        compiler_params=pltpu.CompilerParams(vmem_limit_bytes=40 << 20),
        cost_estimate=work(4 * sum(left.shape[0] for left in lefts) * split * columns, 1),
        name="weight_grad",
    )(*lefts, *rights)


def adam_update(weight, gradient, moment, square, clip_factor):
    clipped = gradient * clip_factor
    moment_new = BETA_ONE * moment + (1.0 - BETA_ONE) * clipped
    square_new = BETA_TWO * square + (1.0 - BETA_TWO) * clipped * clipped
    mean_hat = moment_new / (1.0 - BETA_ONE**STEP)
    square_hat = square_new / (1.0 - BETA_TWO**STEP)
    weight_new = weight - LEARN_RATE * (
        mean_hat / (jnp.sqrt(square_hat) + EPS_ADAM) + WEIGHT_DECAY * weight
    )
    return (weight_new, moment_new, square_new)


def on_device(
    dp,
    tp,
    tokens,
    conditioning,
    out_grad,
    qkv_weight,
    out_weight,
    up_weight,
    down_weight,
    ada_weight,
    qkv_moment,
    out_moment,
    up_moment,
    down_moment,
    ada_moment,
    qkv_square,
    out_square,
    up_square,
    down_square,
    ada_square,
):
    width = tokens.shape[-1]
    heads_width = out_weight.shape[-1]
    here = lax.axis_index("dp")
    select = selection(here, dp, width)
    low_bits = bit_count(dp)
    high_bits = range(1, bit_count(tp))
    chunks = range(tp // 2)

    def swap(value, bit):
        return flip(value, "tensor", tp, bit)

    def widen(value):
        return jnp.concatenate([value, swap(value, 0)], axis=0)

    def all_blocks(value):
        pieces = [value]
        for bit in reversed(high_bits):
            pieces = pieces + [swap(piece, bit) for piece in pieces]
        return pieces

    def token_sum(kept, sent):
        return high_sum([keep + swap(send, 0).astype(WIDE) for keep, send in zip(kept, sent)])

    def high_sum(part):
        for bit in high_bits:
            low_part = [value.astype(LOW) for value in part]
            moved = [swap(value, bit) for value in low_part]
            part = [
                low_part[k].astype(WIDE) + moved[k ^ (1 << (bit - 1))].astype(WIDE) for k in chunks
            ]
        return part

    def split_product(left, right, dims):
        rows = left.shape[0] // 2
        return pin(matmul(left[:rows], right, dims), matmul(left[rows:], right, dims).astype(LOW))

    signal, silu_back = jax.vjp(jax.nn.silu, conditioning)
    low_ada = ada_weight.astype(LOW)
    high, middle_bits = low_bits - 1, list(reversed(range(1, low_bits - 1)))

    def grow_all(value, bits):
        for bit in bits:
            value = grow(value, "dp", dp, bit)
        return value

    signal_all = grow(signal.astype(LOW), "dp", dp, high)
    full_qkv = jnp.concatenate([qkv_weight[t].astype(LOW) for t in range(3)], axis=1)
    signal_all, full_qkv = pin(signal_all, full_qkv)
    full_qkv = grow(full_qkv, "dp", dp, high)
    own_tokens = matmul(tokens[0], select, ((1,), (0,))).astype(LOW)
    own_grad = matmul(out_grad[0], select, ((1,), (0,))).astype(LOW)
    signal_all = grow_all(signal_all, middle_bits + [0])
    tokens_low = all_blocks(own_tokens)
    modulation = jnp.einsum("pi,kni->pkn", signal_all, low_ada, preferred_element_type=WIDE)
    modulation, full_qkv = pin(modulation, full_qkv)
    full_qkv = grow_all(full_qkv, middle_bits)
    modulation = sum_all(modulation, "tensor", tp)
    count = modulation.shape[0] // 2
    moved = flip(modulation[count:], "dp", dp, 0)
    modulation = jnp.concatenate([modulation[:count], moved], axis=-1)
    modulation, full_qkv, tokens_low, own_grad = pin(modulation, full_qkv, tokens_low, own_grad)
    full_qkv = grow(full_qkv, "dp", dp, 0)
    tokens_low = [widen(piece) for piece in tokens_low]
    for bit in [high] + middle_bits:
        modulation = spread_features(modulation, "dp", dp, bit)
    piece = width // dp
    modulation = jnp.concatenate(
        [
            modulation[0, :, (2 * k + low_bit) * piece : (2 * k + low_bit + 1) * piece]
            for low_bit in range(2)
            for k in range(dp // 2)
        ],
        axis=-1,
    )
    modulation = modulation.reshape(6, 1, width)
    shift_one, scale_one, gate_one, shift_two, scale_two, gate_two = modulation

    tokens_wide = [value.astype(WIDE) for value in tokens_low]
    norm_one, inverse_one = zip(*(pin(*normalize(value)) for value in tokens_wide))
    normed_one = [(value * (1.0 + scale_one) + shift_one).astype(LOW) for value in norm_one]
    normed_one = jnp.concatenate(normed_one, axis=0)
    lows = [weight.astype(LOW) for weight in (out_weight, up_weight, down_weight)]
    normed_one, own_grad, (full_out, full_up, full_down) = pin(normed_one, own_grad, lows)
    grad_low = all_blocks(own_grad)
    full_out = grow(full_out, "dp", dp, high)
    full_out, full_up = pin(full_out, full_up)
    full_out = grow_all(full_out, middle_bits)
    full_up = grow(full_up, "dp", dp, high)
    full_qkv, full_out, full_down = pin(full_qkv, full_out, full_down)
    full_out = grow(full_out, "dp", dp, 0)
    full_down = grow(full_down, "dp", dp, high)
    projected = matmul(normed_one, full_qkv, ((1,), (0,))).astype(LOW)
    length = projected.shape[0]
    chunk_rows = length // len(chunks)
    attended, log_totals, part = [], [], []
    for k in chunks:
        mixed, log_total = attend(projected, k, chunk_rows)
        if k == 0:
            mixed, full_out, full_up, full_down = pin(mixed, full_out, full_up, full_down)
            full_down = grow_all(full_down, middle_bits)
            full_up = grow_all(full_up, middle_bits[:-1] + [0])
        keep, send = split_product(mixed, full_out, ((1,), (1,)))
        part.append(keep + swap(send, 0).astype(WIDE))
        part[k], projected = pin(part[k], projected)
        attended.append(mixed)
        log_totals.append(log_total)
    part, full_up, full_down = pin(part, full_up, full_down)
    moved_up = flip(full_up, "dp", dp, middle_bits[-1])
    moved_down = flip(full_down, "dp", dp, 0)
    attn_rows = high_sum(part)
    attn_rows, moved_up, moved_down, grad_low = pin(attn_rows, moved_up, moved_down, grad_low)
    grad_low = [widen(piece) for piece in grad_low]
    own_rows = attn_rows[0].shape[0]
    middle = [tokens_wide[k][:own_rows] + gate_one * attn_rows[k] for k in chunks]
    norm_two, inverse_two = zip(*(normalize(value) for value in middle))
    normed_two = [(value * (1.0 + scale_two) + shift_two).astype(LOW) for value in norm_two]
    seq_two = [widen(value) for value in normed_two]
    rows = full_up.shape[0] // 2
    full_up = jnp.concatenate(
        [full_up[:rows], moved_up[:rows], full_up[rows:], moved_up[rows:]], axis=0
    )
    full_down = jnp.concatenate([full_down, moved_down], axis=0)

    pre_act = [matmul(part, full_up, ((1,), (0,))) for part in seq_two]
    activated, gelu_back = zip(*(jax.vjp(gelu_tanh, part) for part in pre_act))
    hidden = [part.astype(LOW) for part in activated]

    grad_mlp = [(part.astype(WIDE) * gate_two).astype(LOW) for part in grad_low]
    kept_down, sent_down = weight_grad(grad_mlp, hidden)
    kept_down, sent_down, grad_mlp, hidden = pin(kept_down, sent_down, grad_mlp, hidden)
    sent_down = flip(sent_down, "dp", dp, 0)
    grad_hidden = [matmul(part, full_down, ((1,), (0,))) for part in grad_mlp]
    grad_pre = [back(part)[0].astype(LOW) for back, part in zip(gelu_back, grad_hidden)]
    part = []
    for k in chunks:
        keep, send = split_product(grad_pre[k], full_up, ((1,), (1,)))
        part.append(keep + swap(send, 0).astype(WIDE))
    part, grad_pre, seq_two = pin(part, grad_pre, seq_two)
    kept_up, sent_up = weight_grad(seq_two, grad_pre, 2)
    grad_normed_two = high_sum(part)
    grad_normed_two[0], kept_up, sent_up, sent_down = pin(
        grad_normed_two[0], kept_up, sent_up, sent_down
    )
    grad_down = kept_down + sent_down.astype(WIDE)
    for bit in range(1, low_bits - 1):
        grad_down = shrink(grad_down, "dp", dp, bit)

    grad_shift_two = jnp.sum(grad_normed_two[0], axis=0)
    grad_scale_two = jnp.sum(grad_normed_two[0] * norm_two[0], axis=0)
    grad_middle = [
        grad_low[k][:own_rows].astype(WIDE)
        + normalize_back(norm_two[k], inverse_two[k], grad_normed_two[k] * (1.0 + scale_two))
        for k in chunks
    ]
    grad_gate_one = jnp.sum(grad_middle[0] * attn_rows[0], axis=0)

    grad_attn = [widen((part * gate_one).astype(LOW)) for part in grad_middle]
    grad_attended = [
        matmul(part, full_out, ((1,), (0,))).astype(LOW)
        for part in grad_attn
    ]
    kept_out, sent_out = weight_grad(grad_attn, attended)
    kept_out, sent_out, grad_attended = pin(kept_out, sent_out, grad_attended)
    sent_up = flip(sent_up, "dp", dp, 1)
    sent_out = flip(sent_out, "dp", dp, 0)
    grad_projected = attend_back(
        projected, jnp.concatenate(log_totals, axis=1), jnp.concatenate(grad_attended, axis=0)
    )

    grad_projected, sent_out, grad_down = pin(grad_projected, sent_out, grad_down)
    summed_down = shrink(grad_down, "dp", dp, high)
    grad_out = kept_out + sent_out.astype(WIDE)
    kept_qkv, sent_qkv = weight_grad([normed_one], [grad_projected])
    kept_qkv, sent_qkv, grad_projected, hidden = pin(kept_qkv, sent_qkv, grad_projected, hidden)
    sent_qkv = flip(sent_qkv, "dp", dp, 0)
    mlp_kept, mlp_sent = zip(*(split_product(part, full_down, ((1,), (1,))) for part in hidden))
    mlp_part = [keep + swap(send, 0).astype(WIDE) for keep, send in zip(mlp_kept, mlp_sent)]
    mlp_part, grad_projected = pin(mlp_part, grad_projected)
    for bit in high_bits:
        mlp_part = [
            mlp_part[2 * k] + swap(mlp_part[2 * k + 1].astype(LOW), bit).astype(WIDE)
            for k in range(len(mlp_part) // 2)
        ]
    mlp_rows = mlp_part[0]
    block_out = (middle[0] + gate_two * mlp_rows).astype(LOW)
    block_out = matmul(block_out, select, ((1,), (1,))).astype(LOW)
    grad_gate_two = jnp.sum(own_grad.astype(WIDE) * mlp_rows, axis=0)
    one_terms, one_sums = zip(
        *(token_terms(grad_projected, full_qkv, norm_one[k], k) for k in chunks)
    )
    rest = jnp.stack([grad_gate_one, grad_shift_two, grad_scale_two, grad_gate_two])
    one_sums, one_terms, sent_qkv, rest, sent_up, grad_out = pin(
        one_sums, one_terms, sent_qkv, rest, sent_up, grad_out
    )
    for bit in range(1, low_bits - 1):
        grad_out = shrink(grad_out, "dp", dp, bit)
    grad_up = kept_up + sent_up.astype(WIDE)
    grad_up = shrink(grad_up, "dp", dp, 0)
    for bit in range(2, low_bits - 1):
        grad_up = shrink(grad_up, "dp", dp, bit)
    one_part = [
        terms[:own_rows] + swap(terms[own_rows:].astype(LOW), 0).astype(WIDE) for terms in one_terms
    ]
    grad_qkv = kept_qkv + sent_qkv.astype(WIDE)
    for bit in range(1, low_bits - 1):
        grad_qkv = shrink(grad_qkv, "dp", dp, bit)
    grad_mod = jnp.concatenate([sum(one_sums), rest], axis=0)
    grad_mod = sum_all(grad_mod, "tensor", tp).astype(LOW)
    grad_mod = fold_features(grad_mod, "dp", dp, [0])
    half = grad_qkv.shape[0] // 2
    kept_qkv, sent_qkv, one_part, grad_mod, block_out, grad_out, summed_down = pin(
        grad_qkv[:half],
        grad_qkv[half:].astype(LOW),
        one_part,
        grad_mod,
        block_out,
        grad_out,
        summed_down,
    )
    summed_out = shrink(grad_out, "dp", dp, high)
    sent_qkv = flip(sent_qkv, "dp", dp, high)
    for bit in high_bits:
        one_part = [
            one_part[2 * k] + swap(one_part[2 * k + 1].astype(LOW), bit).astype(WIDE)
            for k in range(len(one_part) // 2)
        ]
    grad_mod = fold_features(grad_mod, "dp", dp, range(1, low_bits - 1))
    part_total = jnp.sum(summed_down * summed_down)
    sent_qkv, grad_mod, one_part, part_total, grad_up, summed_out = pin(
        sent_qkv, grad_mod, one_part, part_total, grad_up, summed_out
    )
    summed_up = shrink(grad_up, "dp", dp, high)
    part_total = part_total + jnp.sum(summed_out * summed_out)
    grad_qkv = kept_qkv + sent_qkv.astype(WIDE)
    grad_mod = fold_features(grad_mod, "dp", dp, [high])
    summed_ada = jnp.einsum("pkn,pi->kni", grad_mod, signal_all, preferred_element_type=WIDE)
    summed_qkv = jnp.stack(
        [grad_qkv[:, t * heads_width : (t + 1) * heads_width] for t in range(3)], axis=0
    )
    part_total = part_total + jnp.sum(summed_up * summed_up)
    total = part_total + jnp.sum(grad_qkv * grad_qkv) + jnp.sum(summed_ada * summed_ada)

    input_grad = grad_middle[0] + normalize_back(
        norm_one[0][:own_rows], inverse_one[0][:own_rows], one_part[0] * (1.0 + scale_one)
    )
    coarse = input_grad.astype(LOW)
    fine = (input_grad - coarse.astype(WIDE)).astype(LOW)
    input_grad = matmul(coarse, select, ((1,), (1,))) + matmul(fine, select, ((1,), (1,)))
    grad_signal = jnp.einsum("pkn,kni->pi", grad_mod, low_ada, preferred_element_type=WIDE)
    total = sum_all(total, "tensor", tp)
    total, input_grad = pin(total, input_grad)
    for bit in range(low_bits):
        rows = grad_signal.shape[0] // 2
        row = jnp.broadcast_to(total, (1, grad_signal.shape[1]))
        sent = jnp.concatenate([grad_signal[rows:], row], axis=0)
        moved = flip(sent, "dp", dp, bit)
        grad_signal = grad_signal[:rows] + moved[:rows]
        total = total + moved[rows, 0]
    cond_grad = silu_back(grad_signal)[0]
    grad_norm = jnp.sqrt(total)
    clip_factor = CLIP_NORM / jnp.maximum(grad_norm, CLIP_NORM)
    qkv = adam_update(qkv_weight, summed_qkv, qkv_moment, qkv_square, clip_factor)
    out = adam_update(out_weight, summed_out, out_moment, out_square, clip_factor)
    up = adam_update(up_weight, summed_up, up_moment, up_square, clip_factor)
    down = adam_update(down_weight, summed_down, down_moment, down_square, clip_factor)
    ada = adam_update(ada_weight, summed_ada, ada_moment, ada_square, clip_factor)
    return (
        block_out[None],
        input_grad[None],
        cond_grad,
        grad_norm,
        *(new for group in zip(qkv, out, up, down, ada) for new in group),
    )


def solution(mesh):
    dp, tp = mesh.shape["dp"], mesh.shape["tensor"]
    rows = P("dp", "tensor", None)
    plain = P("dp", "tensor")
    stacked = P(None, "dp", "tensor")
    weights = (stacked, plain, plain, plain, stacked)

    def step(*arrays):
        return on_device(dp, tp, *arrays)

    return jax.shard_map(
        step,
        mesh=mesh,
        in_specs=(rows, plain, rows) + weights * 3,
        out_specs=(rows, rows, plain, P()) + weights * 3,
        check_vma=False,
    )
```

```python
import functools

import jax
import jax.numpy as jnp
import numpy as np
from jax import lax
from jax.experimental import pallas as pl
from jax.experimental.pallas import tpu as pltpu
from jax.sharding import PartitionSpec as P

HEAD_DIM = 72
SCORE_SCALE = HEAD_DIM ** (-0.5)
QUERY_ROWS = 256
COLUMN_BLOCK = 384
STEP = 10

EPS_NORM = 1e-06
CLIP_NORM = 1.0
LEARN_RATE = 0.05
WEIGHT_DECAY = 0.1
BETA_ONE = 0.9
BETA_TWO = 0.999
EPS_ADAM = 1e-08

LOW = jnp.bfloat16
WIDE = jnp.float32


def bit_count(size):
    return size.bit_length() - 1


def flip(value, axis, size, bit):
    return lax.ppermute(value, axis, [(i, i ^ (1 << bit)) for i in range(size)])


def grow(value, axis, size, bit):
    return jnp.concatenate([value, flip(value, axis, size, bit)], axis=0)


def shrink(value, axis, size, bit):
    half = value.shape[0] // 2
    moved = flip(value[half:].astype(LOW), axis, size, bit)
    return value[:half] + moved.astype(WIDE)


def gather_rel(value, axis, size):
    for bit in reversed(range(bit_count(size))):
        value = grow(value, axis, size, bit)
    return value


def scatter_rel(value, axis, size):
    for bit in range(bit_count(size)):
        value = shrink(value, axis, size, bit)
    return value


def spread_features(value, axis, size, bit):
    pairs = value.reshape((value.shape[0] // 2, 2) + value.shape[1:])
    moved = flip(pairs[:, 1], axis, size, bit)
    return jnp.concatenate([pairs[:, 0], moved], axis=-1)


def fold_features(value, axis, size, bits):
    if value.ndim == 2:
        value = value[None]
    for bit in bits:
        half = value.shape[-1] // 2
        moved = flip(value[..., half:], axis, size, bit)
        value = jnp.stack([value[..., :half], moved], axis=1)
        value = value.reshape((-1,) + value.shape[2:])
    return value


def sum_all(value, axis, size):
    for bit in range(bit_count(size)):
        value = value + flip(value, axis, size, bit)
    return value


def pin(*values):
    return lax.optimization_barrier(values)


def reversed_bits(size):
    bits = bit_count(size)
    return np.array([int(format(i, f"0{bits}b")[::-1], 2) if bits else 0 for i in range(size)])


def selection(index, size, width):
    block = width // size
    place = np.arange(width)
    source = (index ^ jnp.asarray(reversed_bits(size)[place // block], jnp.int32)) * block
    source = source + jnp.asarray(place % block, jnp.int32)
    return (lax.broadcasted_iota(jnp.int32, (width, width), 0) == source[None, :]).astype(LOW)


def matmul(left, right, dims):
    return lax.dot_general(left, right, (dims, ((), ())), preferred_element_type=WIDE)


def normalize(values):
    centre = values - jnp.mean(values, axis=-1, keepdims=True)
    spread = jnp.mean(centre * centre, axis=-1, keepdims=True)
    inverse = lax.rsqrt(spread + EPS_NORM)
    return centre * inverse, inverse


def normalize_back(normed, inverse, grad):
    mean_grad = jnp.mean(grad, axis=-1, keepdims=True)
    mean_both = jnp.mean(grad * normed, axis=-1, keepdims=True)
    return inverse * (grad - mean_grad - normed * mean_both)


def gelu_tanh(values):
    return jax.nn.gelu(values, approximate=True)


def work(flops, weight):
    return pl.CostEstimate(flops=weight * flops, bytes_accessed=1 << 20, transcendentals=0)


def attend_kernel(query_ref, all_ref, out_ref, log_ref):
    heads_width = out_ref.shape[1]
    for head in range(heads_width // HEAD_DIM):
        place = head * HEAD_DIM
        queries = query_ref[:, place : place + HEAD_DIM]
        keys = all_ref[:, heads_width + place : heads_width + place + HEAD_DIM]
        values = all_ref[:, 2 * heads_width + place : 2 * heads_width + place + HEAD_DIM]
        scores = matmul(keys, queries, ((1,), (1,)))
        peak = jnp.max(scores, axis=0, keepdims=True)
        exponent = jnp.exp((scores - peak) * SCORE_SCALE)
        total = jnp.sum(exponent, axis=0, keepdims=True)
        probability = (exponent * (1.0 / total)).astype(LOW)
        mixture = matmul(values, probability, ((0,), (0,)))
        out_ref[:, place : place + HEAD_DIM] = mixture.T.astype(LOW)
        log_ref[head : head + 1, :] = peak * SCORE_SCALE + jnp.log(total)


def attend(projected, chunk, chunk_rows):
    length, all_width = projected.shape
    heads_width = all_width // 3
    rows = min(QUERY_ROWS, chunk_rows)
    start = chunk * chunk_rows // rows
    return pl.pallas_call(
        attend_kernel,
        grid=(chunk_rows // rows,),
        in_specs=[
            pl.BlockSpec((rows, all_width), lambda i: (start + i, 0)),
            pl.BlockSpec((length, all_width), lambda i: (0, 0)),
        ],
        out_specs=[
            pl.BlockSpec((rows, heads_width), lambda i: (i, 0)),
            pl.BlockSpec((heads_width // HEAD_DIM, rows), lambda i: (0, i)),
        ],
        out_shape=[
            jax.ShapeDtypeStruct((chunk_rows, heads_width), LOW),
            jax.ShapeDtypeStruct((heads_width // HEAD_DIM, chunk_rows), WIDE),
        ],
        compiler_params=pltpu.CompilerParams(vmem_limit_bytes=24 << 20),
        cost_estimate=work(4 * chunk_rows * length * heads_width, 4),
        name="attend",
    )(projected, projected)


def attend_back_kernel(query_ref, all_ref, log_ref, grad_ref, out_ref, key_sum, value_sum):
    heads_width = grad_ref.shape[1]
    rows = query_ref.shape[0]
    step = pl.program_id(0)

    @pl.when(step == 0)
    def _():
        key_sum[...] = jnp.zeros_like(key_sum)
        value_sum[...] = jnp.zeros_like(value_sum)

    for head in range(heads_width // HEAD_DIM):
        place = head * HEAD_DIM
        queries = query_ref[:, place : place + HEAD_DIM]
        keys = all_ref[:, heads_width + place : heads_width + place + HEAD_DIM]
        values = all_ref[:, 2 * heads_width + place : 2 * heads_width + place + HEAD_DIM]
        grads = grad_ref[:, place : place + HEAD_DIM]
        scores = matmul(keys, queries, ((1,), (1,)))
        probability = jnp.exp(scores * SCORE_SCALE - log_ref[head : head + 1, :])
        grad_probability = matmul(values, grads, ((1,), (1,)))
        inner = jnp.sum(probability * grad_probability, axis=0, keepdims=True)
        grad_scores = (probability * (grad_probability - inner)).astype(LOW)
        key_sum[head] += matmul(grad_scores, queries, ((1,), (0,)))
        value_sum[head] += matmul(probability.astype(LOW), grads, ((1,), (0,)))
        grad_query = matmul(keys, grad_scores, ((0,), (0,))) * SCORE_SCALE
        out_ref[pl.ds(pl.multiple_of(step * rows, rows), rows), place : place + HEAD_DIM] = (
            grad_query.T.astype(LOW)
        )

    @pl.when(step == pl.num_programs(0) - 1)
    def _():
        for head in range(heads_width // HEAD_DIM):
            place = heads_width + head * HEAD_DIM
            out_ref[:, place : place + HEAD_DIM] = (key_sum[head] * SCORE_SCALE).astype(LOW)
            place += heads_width
            out_ref[:, place : place + HEAD_DIM] = value_sum[head].astype(LOW)


def attend_back(projected, log_totals, grad_attended):
    length, all_width = projected.shape
    heads_width = all_width // 3
    heads = heads_width // HEAD_DIM
    rows = min(QUERY_ROWS, length)
    return pl.pallas_call(
        attend_back_kernel,
        grid=(length // rows,),
        in_specs=[
            pl.BlockSpec((rows, all_width), lambda i: (i, 0)),
            pl.BlockSpec((length, all_width), lambda i: (0, 0)),
            pl.BlockSpec((heads, rows), lambda i: (0, i)),
            pl.BlockSpec((rows, heads_width), lambda i: (i, 0)),
        ],
        out_specs=pl.BlockSpec((length, all_width), lambda i: (0, 0)),
        out_shape=jax.ShapeDtypeStruct((length, all_width), LOW),
        scratch_shapes=[
            pltpu.VMEM((heads, length, HEAD_DIM), WIDE),
            pltpu.VMEM((heads, length, HEAD_DIM), WIDE),
        ],
        compiler_params=pltpu.CompilerParams(vmem_limit_bytes=36 << 20),
        cost_estimate=work(10 * length * length * heads_width, 2),
        name="attend_back",
    )(projected, projected, log_totals, grad_attended)


def token_terms_kernel(grad_ref, weight_ref, norm_ref, terms_ref, sums_ref):
    terms = matmul(grad_ref[...], weight_ref[...], ((1,), (1,)))
    terms_ref[...] = terms

    @pl.when(pl.program_id(0) == 0)
    def _():
        sums_ref[...] = jnp.zeros_like(sums_ref)

    sums_ref[0:1] += jnp.sum(terms, axis=0, keepdims=True)
    sums_ref[1:2] += jnp.sum(terms * norm_ref[...], axis=0, keepdims=True)


def token_terms(grads, weight, normed, chunk):
    chunk_rows, width = normed.shape
    rows = min(QUERY_ROWS, chunk_rows)
    start = chunk * chunk_rows // rows
    return pl.pallas_call(
        token_terms_kernel,
        grid=(chunk_rows // rows,),
        in_specs=[
            pl.BlockSpec((rows, grads.shape[1]), lambda i: (start + i, 0)),
            pl.BlockSpec(weight.shape, lambda i: (0, 0)),
            pl.BlockSpec((rows, width), lambda i: (i, 0)),
        ],
        out_specs=[
            pl.BlockSpec((rows, width), lambda i: (i, 0)),
            pl.BlockSpec((2, width), lambda i: (0, 0)),
        ],
        out_shape=[
            jax.ShapeDtypeStruct((chunk_rows, width), WIDE),
            jax.ShapeDtypeStruct((2, width), WIDE),
        ],
        compiler_params=pltpu.CompilerParams(vmem_limit_bytes=24 << 20),
        cost_estimate=work(2 * chunk_rows * width * grads.shape[1], 1),
        name="token_terms",
    )(grads, weight, normed)


def weight_grad_kernel(pairs, *refs):
    parts = (len(refs) - 2) // 2
    lefts, rights, (kept_ref, sent_ref) = refs[:parts], refs[parts:-2], refs[-2:]
    split, columns = kept_ref.shape
    turned = [left[...].T for left in lefts]
    for start in range(0, columns, COLUMN_BLOCK):
        stop = min(start + COLUMN_BLOCK, columns)
        total = sum(
            matmul(left, right[:, start:stop], ((1,), (0,))) for left, right in zip(turned, rights)
        )
        rows = split // pairs
        for k in range(pairs):
            place = slice(k * rows, (k + 1) * rows)
            kept_ref[place, start:stop] = total[2 * k * rows : (2 * k + 1) * rows]
            sent_ref[place, start:stop] = total[(2 * k + 1) * rows : (2 * k + 2) * rows].astype(LOW)


def weight_grad(lefts, rights, pairs=1):
    split, columns = lefts[0].shape[1] // 2, rights[0].shape[1]
    return pl.pallas_call(
        functools.partial(weight_grad_kernel, pairs),
        out_shape=[
            jax.ShapeDtypeStruct((split, columns), WIDE),
            jax.ShapeDtypeStruct((split, columns), LOW),
        ],
        compiler_params=pltpu.CompilerParams(vmem_limit_bytes=40 << 20),
        cost_estimate=work(4 * sum(left.shape[0] for left in lefts) * split * columns, 1),
        name="weight_grad",
    )(*lefts, *rights)


def adam_update(weight, gradient, moment, square, clip_factor):
    clipped = gradient * clip_factor
    moment_new = BETA_ONE * moment + (1.0 - BETA_ONE) * clipped
    square_new = BETA_TWO * square + (1.0 - BETA_TWO) * clipped * clipped
    mean_hat = moment_new / (1.0 - BETA_ONE**STEP)
    square_hat = square_new / (1.0 - BETA_TWO**STEP)
    weight_new = weight - LEARN_RATE * (
        mean_hat / (jnp.sqrt(square_hat) + EPS_ADAM) + WEIGHT_DECAY * weight
    )
    return (weight_new, moment_new, square_new)


def on_device(
    dp,
    tp,
    tokens,
    conditioning,
    out_grad,
    qkv_weight,
    out_weight,
    up_weight,
    down_weight,
    ada_weight,
    qkv_moment,
    out_moment,
    up_moment,
    down_moment,
    ada_moment,
    qkv_square,
    out_square,
    up_square,
    down_square,
    ada_square,
):
    width = tokens.shape[-1]
    heads_width = out_weight.shape[-1]
    here = lax.axis_index("dp")
    select = selection(here, dp, width)
    low_bits = bit_count(dp)
    high_bits = range(1, bit_count(tp))
    chunks = range(tp // 2)

    def swap(value, bit):
        return flip(value, "tensor", tp, bit)

    def widen(value):
        return jnp.concatenate([value, swap(value, 0)], axis=0)

    def all_blocks(value):
        pieces = [value]
        for bit in reversed(high_bits):
            pieces = pieces + [swap(piece, bit) for piece in pieces]
        return pieces

    def token_sum(kept, sent):
        return high_sum([keep + swap(send, 0).astype(WIDE) for keep, send in zip(kept, sent)])

    def high_sum(part):
        for bit in high_bits:
            low_part = [value.astype(LOW) for value in part]
            moved = [swap(value, bit) for value in low_part]
            part = [
                low_part[k].astype(WIDE) + moved[k ^ (1 << (bit - 1))].astype(WIDE) for k in chunks
            ]
        return part

    def split_product(left, right, dims):
        rows = left.shape[0] // 2
        return pin(matmul(left[:rows], right, dims), matmul(left[rows:], right, dims).astype(LOW))

    signal, silu_back = jax.vjp(jax.nn.silu, conditioning)
    low_ada = ada_weight.astype(LOW)
    high, middle_bits = low_bits - 1, list(reversed(range(1, low_bits - 1)))

    def grow_all(value, bits):
        for bit in bits:
            value = grow(value, "dp", dp, bit)
        return value

    signal_all = grow(signal.astype(LOW), "dp", dp, high)
    full_qkv = jnp.concatenate([qkv_weight[t].astype(LOW) for t in range(3)], axis=1)
    signal_all, full_qkv = pin(signal_all, full_qkv)
    full_qkv = grow(full_qkv, "dp", dp, high)
    own_tokens = matmul(tokens[0], select, ((1,), (0,))).astype(LOW)
    own_grad = matmul(out_grad[0], select, ((1,), (0,))).astype(LOW)
    signal_all = grow_all(signal_all, middle_bits + [0])
    tokens_low = all_blocks(own_tokens)
    modulation = jnp.einsum("pi,kni->pkn", signal_all, low_ada, preferred_element_type=WIDE)
    modulation, full_qkv = pin(modulation, full_qkv)
    full_qkv = grow_all(full_qkv, middle_bits)
    modulation = sum_all(modulation, "tensor", tp)
    count = modulation.shape[0] // 2
    moved = flip(modulation[count:], "dp", dp, 0)
    modulation = jnp.concatenate([modulation[:count], moved], axis=-1)
    modulation, full_qkv, tokens_low, own_grad = pin(modulation, full_qkv, tokens_low, own_grad)
    full_qkv = grow(full_qkv, "dp", dp, 0)
    tokens_low = [widen(piece) for piece in tokens_low]
    for bit in [high] + middle_bits:
        modulation = spread_features(modulation, "dp", dp, bit)
    piece = width // dp
    modulation = jnp.concatenate(
        [
            modulation[0, :, (2 * k + low_bit) * piece : (2 * k + low_bit + 1) * piece]
            for low_bit in range(2)
            for k in range(dp // 2)
        ],
        axis=-1,
    )
    modulation = modulation.reshape(6, 1, width)
    shift_one, scale_one, gate_one, shift_two, scale_two, gate_two = modulation

    tokens_wide = [value.astype(WIDE) for value in tokens_low]
    norm_one, inverse_one = zip(*(pin(*normalize(value)) for value in tokens_wide))
    normed_one = [(value * (1.0 + scale_one) + shift_one).astype(LOW) for value in norm_one]
    normed_one = jnp.concatenate(normed_one, axis=0)
    lows = [weight.astype(LOW) for weight in (out_weight, up_weight, down_weight)]
    normed_one, own_grad, (full_out, full_up, full_down) = pin(normed_one, own_grad, lows)
    grad_low = all_blocks(own_grad)
    full_out = grow(full_out, "dp", dp, high)
    full_out, full_up = pin(full_out, full_up)
    full_out = grow_all(full_out, middle_bits)
    full_up = grow(full_up, "dp", dp, high)
    full_qkv, full_out, full_down = pin(full_qkv, full_out, full_down)
    full_out = grow(full_out, "dp", dp, 0)
    full_down = grow(full_down, "dp", dp, high)
    projected = matmul(normed_one, full_qkv, ((1,), (0,))).astype(LOW)
    length = projected.shape[0]
    chunk_rows = length // len(chunks)
    attended, log_totals, part = [], [], []
    for k in chunks:
        mixed, log_total = attend(projected, k, chunk_rows)
        if k == 0:
            mixed, full_out, full_up, full_down = pin(mixed, full_out, full_up, full_down)
            full_down = grow_all(full_down, middle_bits)
            full_up = grow_all(full_up, middle_bits[:-1] + [0])
        keep, send = split_product(mixed, full_out, ((1,), (1,)))
        part.append(keep + swap(send, 0).astype(WIDE))
        part[k], projected = pin(part[k], projected)
        attended.append(mixed)
        log_totals.append(log_total)
    part, full_up, full_down = pin(part, full_up, full_down)
    moved_up = flip(full_up, "dp", dp, middle_bits[-1])
    moved_down = flip(full_down, "dp", dp, 0)
    attn_rows = high_sum(part)
    attn_rows, moved_up, moved_down, grad_low = pin(attn_rows, moved_up, moved_down, grad_low)
    grad_low = [widen(piece) for piece in grad_low]
    own_rows = attn_rows[0].shape[0]
    middle = [tokens_wide[k][:own_rows] + gate_one * attn_rows[k] for k in chunks]
    norm_two, inverse_two = zip(*(normalize(value) for value in middle))
    normed_two = [(value * (1.0 + scale_two) + shift_two).astype(LOW) for value in norm_two]
    seq_two = [widen(value) for value in normed_two]
    rows = full_up.shape[0] // 2
    full_up = jnp.concatenate(
        [full_up[:rows], moved_up[:rows], full_up[rows:], moved_up[rows:]], axis=0
    )
    full_down = jnp.concatenate([full_down, moved_down], axis=0)

    pre_act = [matmul(part, full_up, ((1,), (0,))) for part in seq_two]
    activated, gelu_back = zip(*(jax.vjp(gelu_tanh, part) for part in pre_act))
    hidden = [part.astype(LOW) for part in activated]

    grad_mlp = [(part.astype(WIDE) * gate_two).astype(LOW) for part in grad_low]
    kept_down, sent_down = weight_grad(grad_mlp, hidden)
    kept_down, sent_down, grad_mlp, hidden = pin(kept_down, sent_down, grad_mlp, hidden)
    sent_down = flip(sent_down, "dp", dp, 0)
    grad_hidden = [matmul(part, full_down, ((1,), (0,))) for part in grad_mlp]
    grad_pre = [back(part)[0].astype(LOW) for back, part in zip(gelu_back, grad_hidden)]
    part = []
    for k in chunks:
        keep, send = split_product(grad_pre[k], full_up, ((1,), (1,)))
        part.append(keep + swap(send, 0).astype(WIDE))
    part, grad_pre, seq_two = pin(part, grad_pre, seq_two)
    kept_up, sent_up = weight_grad(seq_two, grad_pre, 2)
    grad_normed_two = high_sum(part)
    grad_normed_two[0], kept_up, sent_up, sent_down = pin(
        grad_normed_two[0], kept_up, sent_up, sent_down
    )
    grad_down = kept_down + sent_down.astype(WIDE)
    for bit in range(1, low_bits - 1):
        grad_down = shrink(grad_down, "dp", dp, bit)

    grad_shift_two = jnp.sum(grad_normed_two[0], axis=0)
    grad_scale_two = jnp.sum(grad_normed_two[0] * norm_two[0], axis=0)
    grad_middle = [
        grad_low[k][:own_rows].astype(WIDE)
        + normalize_back(norm_two[k], inverse_two[k], grad_normed_two[k] * (1.0 + scale_two))
        for k in chunks
    ]
    grad_gate_one = jnp.sum(grad_middle[0] * attn_rows[0], axis=0)

    grad_attn = [widen((part * gate_one).astype(LOW)) for part in grad_middle]
    grad_attended = [
        matmul(part, full_out, ((1,), (0,))).astype(LOW)
        for part in grad_attn
    ]
    kept_out, sent_out = weight_grad(grad_attn, attended)
    kept_out, sent_out, grad_attended = pin(kept_out, sent_out, grad_attended)
    sent_up = flip(sent_up, "dp", dp, 1)
    sent_out = flip(sent_out, "dp", dp, 0)
    grad_projected = attend_back(
        projected, jnp.concatenate(log_totals, axis=1), jnp.concatenate(grad_attended, axis=0)
    )

    grad_projected, sent_out, grad_down = pin(grad_projected, sent_out, grad_down)
    summed_down = shrink(grad_down, "dp", dp, high)
    grad_out = kept_out + sent_out.astype(WIDE)
    kept_qkv, sent_qkv = weight_grad([normed_one], [grad_projected])
    kept_qkv, sent_qkv, grad_projected, hidden = pin(kept_qkv, sent_qkv, grad_projected, hidden)
    sent_qkv = flip(sent_qkv, "dp", dp, 0)
    mlp_kept, mlp_sent = zip(*(split_product(part, full_down, ((1,), (1,))) for part in hidden))
    mlp_part = [keep + swap(send, 0).astype(WIDE) for keep, send in zip(mlp_kept, mlp_sent)]
    mlp_part, grad_projected = pin(mlp_part, grad_projected)
    for bit in high_bits:
        mlp_part = [
            mlp_part[2 * k] + swap(mlp_part[2 * k + 1].astype(LOW), bit).astype(WIDE)
            for k in range(len(mlp_part) // 2)
        ]
    mlp_rows = mlp_part[0]
    block_out = (middle[0] + gate_two * mlp_rows).astype(LOW)
    block_out = matmul(block_out, select, ((1,), (1,))).astype(LOW)
    grad_gate_two = jnp.sum(own_grad.astype(WIDE) * mlp_rows, axis=0)
    one_terms, one_sums = zip(
        *(token_terms(grad_projected, full_qkv, norm_one[k], k) for k in chunks)
    )
    rest = jnp.stack([grad_gate_one, grad_shift_two, grad_scale_two, grad_gate_two])
    one_sums, one_terms, sent_qkv, rest, sent_up, grad_out = pin(
        one_sums, one_terms, sent_qkv, rest, sent_up, grad_out
    )
    for bit in range(1, low_bits - 1):
        grad_out = shrink(grad_out, "dp", dp, bit)
    grad_up = kept_up + sent_up.astype(WIDE)
    grad_up = shrink(grad_up, "dp", dp, 0)
    for bit in range(2, low_bits - 1):
        grad_up = shrink(grad_up, "dp", dp, bit)
    one_part = [
        terms[:own_rows] + swap(terms[own_rows:].astype(LOW), 0).astype(WIDE) for terms in one_terms
    ]
    grad_qkv = kept_qkv + sent_qkv.astype(WIDE)
    for bit in range(1, low_bits - 1):
        grad_qkv = shrink(grad_qkv, "dp", dp, bit)
    grad_mod = jnp.concatenate([sum(one_sums), rest], axis=0)
    grad_mod = sum_all(grad_mod, "tensor", tp).astype(LOW)
    grad_mod = fold_features(grad_mod, "dp", dp, [0])
    half = grad_qkv.shape[0] // 2
    kept_qkv, sent_qkv, one_part, grad_mod, block_out, grad_out, summed_down = pin(
        grad_qkv[:half],
        grad_qkv[half:].astype(LOW),
        one_part,
        grad_mod,
        block_out,
        grad_out,
        summed_down,
    )
    sent_qkv = flip(sent_qkv, "dp", dp, high)
    for bit in high_bits:
        one_part = [
            one_part[2 * k] + swap(one_part[2 * k + 1].astype(LOW), bit).astype(WIDE)
            for k in range(len(one_part) // 2)
        ]
    grad_mod = fold_features(grad_mod, "dp", dp, range(1, low_bits - 1))
    part_total = jnp.sum(summed_down * summed_down)
    sent_qkv, grad_mod, one_part, part_total, grad_up, grad_out = pin(
        sent_qkv, grad_mod, one_part, part_total, grad_up, grad_out
    )
    summed_out = shrink(grad_out, "dp", dp, high)
    summed_up = shrink(grad_up, "dp", dp, high)
    part_total = part_total + jnp.sum(summed_out * summed_out)
    grad_qkv = kept_qkv + sent_qkv.astype(WIDE)
    grad_mod = fold_features(grad_mod, "dp", dp, [high])
    summed_ada = jnp.einsum("pkn,pi->kni", grad_mod, signal_all, preferred_element_type=WIDE)
    summed_qkv = jnp.stack(
        [grad_qkv[:, t * heads_width : (t + 1) * heads_width] for t in range(3)], axis=0
    )
    part_total = part_total + jnp.sum(summed_up * summed_up)
    total = part_total + jnp.sum(grad_qkv * grad_qkv) + jnp.sum(summed_ada * summed_ada)

    input_grad = grad_middle[0] + normalize_back(
        norm_one[0][:own_rows], inverse_one[0][:own_rows], one_part[0] * (1.0 + scale_one)
    )
    coarse = input_grad.astype(LOW)
    fine = (input_grad - coarse.astype(WIDE)).astype(LOW)
    input_grad = matmul(coarse, select, ((1,), (1,))) + matmul(fine, select, ((1,), (1,)))
    grad_signal = jnp.einsum("pkn,kni->pi", grad_mod, low_ada, preferred_element_type=WIDE)
    total = sum_all(total, "tensor", tp)
    total, input_grad = pin(total, input_grad)
    for bit in range(low_bits):
        rows = grad_signal.shape[0] // 2
        row = jnp.broadcast_to(total, (1, grad_signal.shape[1]))
        sent = jnp.concatenate([grad_signal[rows:], row], axis=0)
        moved = flip(sent, "dp", dp, bit)
        grad_signal = grad_signal[:rows] + moved[:rows]
        total = total + moved[rows, 0]
    cond_grad = silu_back(grad_signal)[0]
    grad_norm = jnp.sqrt(total)
    clip_factor = CLIP_NORM / jnp.maximum(grad_norm, CLIP_NORM)
    qkv = adam_update(qkv_weight, summed_qkv, qkv_moment, qkv_square, clip_factor)
    out = adam_update(out_weight, summed_out, out_moment, out_square, clip_factor)
    up = adam_update(up_weight, summed_up, up_moment, up_square, clip_factor)
    down = adam_update(down_weight, summed_down, down_moment, down_square, clip_factor)
    ada = adam_update(ada_weight, summed_ada, ada_moment, ada_square, clip_factor)
    return (
        block_out[None],
        input_grad[None],
        cond_grad,
        grad_norm,
        *(new for group in zip(qkv, out, up, down, ada) for new in group),
    )


def solution(mesh):
    dp, tp = mesh.shape["dp"], mesh.shape["tensor"]
    rows = P("dp", "tensor", None)
    plain = P("dp", "tensor")
    stacked = P(None, "dp", "tensor")
    weights = (stacked, plain, plain, plain, stacked)

    def step(*arrays):
        return on_device(dp, tp, *arrays)

    return jax.shard_map(
        step,
        mesh=mesh,
        in_specs=(rows, plain, rows) + weights * 3,
        out_specs=(rows, rows, plain, P()) + weights * 3,
        check_vma=False,
    )
```
